32 devices in a mesh: tm: 8 (over y, x, core), chan: 4 (over z).
Axes of the slice: x: 2, y: 2, z: 4, core: 2. Of those that a mesh axis runs over, the one named last changes fastest.
Arguments:
- frames: bfloat16 [8192, 1280], P('tm', 'chan'), may hold values from -64 to 64
- up_weight: bfloat16 [1280, 5120], P('tm', 'chan'), may hold values from -0.15625 to 0.15625
- down_weight: bfloat16 [5120, 1280], P('chan', 'tm'), may hold values from -0.078125 to 0.078125
- ffn_gain: float32 [1280], replicated, may hold values from 0.1 to 1.9
- final_gain: float32 [1280], replicated, may hold values from 0.5 to 1.5
- ctc_weight: bfloat16 [1280, 256], replicated, may hold values from -12 to 12
- labels: int32 [8192], replicated, may hold values from 0 to 255, as said below
- starts: int32 [32], replicated, may hold values from 0 to 1984, as said below
- widths: int32 [32], replicated, may hold values from 64 to 128
Outputs:
- emissions: float32 [8192, 256], P(('tm', 'chan'))
- band_scores: float32 [32, 128], P(('tm', 'chan'))
The draws below stay inside these ranges and needn't reach their ends.
Inputs may be any that keep to these rules, and one draw needn't show every extreme that they name: `labels`: every even state has id 0. Never falling; starts[0] and each rise from one entry to the next are at most 128; the last entry is the largest.
All inputs are finite; a program needn't handle non-finite values.
Results may differ from the reference program's by a relative error of at most 0.0023.
Values may be sent and summed in bfloat16 or wider, within the bound.
No kernel may reach another device: no remote copies, remote signals or barrier semaphores. Data moves between devices by JAX's collectives and lax.ppermute only.
A program may use at most 64 MiB of HBM per device.

```python
import jax
import jax.numpy as jnp
from jax import lax

D = 1280
FF = 5120
V = 256
S = 8192
BAND = 128
FD = 256
SHARDS = 32
FRAMES = 8192


BLANK_LEAN = 26.0


def common_direction(key):
    return jax.random.normal(jax.random.fold_in(key, 9), (1, D), jnp.float32)


def draw_frames(key, part):
    keys = jax.random.split(jax.random.fold_in(key, 1), 1)
    common = common_direction(key)
    values = jnp.clip(jax.random.normal(keys[0], (FRAMES, D), jnp.float32), -6.0, 6.0) + common
    values = jnp.clip(values, -64.0, 64.0)
    return values.astype(jnp.bfloat16)


def draw_ctc_weight(key, part):
    keys = jax.random.split(jax.random.fold_in(key, 2), 1)
    spread = 3.0 / D ** 0.5
    lean_col = BLANK_LEAN * common_direction(key)[0] / D
    values = jnp.clip(jax.random.normal(keys[0], (D, V), jnp.float32), -6.0, 6.0) * spread
    values = values.at[:, 0].set(lean_col + 0.5 * values[:, 0])
    return values.astype(jnp.bfloat16)


def draw_labels(key, part):
    states = jnp.arange(S, dtype=jnp.int32)
    chars = jax.random.randint(jax.random.fold_in(key, 3), (S,), 1, V, dtype=jnp.int32)
    return jnp.where(states % 2 == 0, 0, chars).astype(jnp.int32)


def draw_starts(key, part):
    top = min(S - 2 * BAND, (SHARDS - 1) * (BAND // 2))
    need = -(-top // BAND)
    flat_most = SHARDS - need
    flat_len = flat_most // 2 + jax.random.randint(jax.random.fold_in(key, 4), (), 0, flat_most // 4 + 1, dtype=jnp.int32)
    flat_len = jnp.maximum(flat_len, 1).astype(jnp.int32)
    first = jax.random.randint(jax.random.fold_in(key, 5), (), 0, BAND // 2 + 1, dtype=jnp.int32)
    first = jnp.minimum(first, top).astype(jnp.int32)
    rising = (SHARDS - flat_len).astype(jnp.int32)
    step_most = (top - first + rising - 1) // rising
    shard_ids = jnp.arange(SHARDS, dtype=jnp.int32)
    since = jnp.maximum(shard_ids - (flat_len - 1), 0)
    base = first + since * (top - first) // rising
    jitter = jax.random.randint(jax.random.fold_in(key, 10), (SHARDS,), 0, BAND - step_most + 1, dtype=jnp.int32)
    jitter = jnp.where((shard_ids < flat_len) | (shard_ids == SHARDS - 1), 0, jitter)
    raised = jnp.minimum(base + jitter, top)
    return jax.lax.cummax(raised, axis=0).astype(jnp.int32)


def draw_widths(key, part):
    values = jax.random.randint(jax.random.fold_in(key, 6), (SHARDS,), BAND // 2, BAND + 1, dtype=jnp.int32)
    forced = jax.random.randint(jax.random.fold_in(key, 8), (), 0, SHARDS, dtype=jnp.int32)
    return jnp.where(jnp.arange(SHARDS, dtype=jnp.int32) == forced, BAND, values).astype(jnp.int32)


def steps_of(rng, shape, shards, smallest, largest):
    loudness = 1.0
    for axis_at, parts in shards:
        heights = jax.random.uniform(jax.random.fold_in(jax.random.fold_in(rng, 6), axis_at), (parts,), jnp.float32, smallest / len(shards), largest / len(shards))
        loudness = loudness * jnp.repeat(jnp.exp(heights), shape[axis_at] // parts).reshape((-1,) + (1,) * (len(shape) - 1 - axis_at))
    return loudness


def scatter_about(rng, dims, deviation, reach, cuts=(), held_as=jnp.bfloat16):
    values = deviation * jax.random.normal(rng, dims, jnp.float32)
    if cuts:
        values = values * steps_of(rng, dims, cuts, -0.22, 0.18)
    return jnp.clip(values, -reach, reach).astype(held_as)


def setup_inputs(seed: int = 0) -> dict:
    splits = jax.random.split(jax.random.key(seed), 10)
    return {
        "frames": draw_frames(jax.random.fold_in(splits[9], 71), 0),
        "up_weight": scatter_about(splits[1], (D, FF), D ** -0.5, 0.15625, ((0, 8), (1, 4))),
        "down_weight": scatter_about(splits[2], (FF, D), FF ** -0.5, 0.078125, ((0, 4), (1, 8))),
        "ffn_gain": jnp.clip(1.0 + 0.18 * jax.random.normal(splits[3], (D,), jnp.float32), 0.1, 1.9),
        "final_gain": jnp.clip(1.0 + 0.1 * jax.random.normal(splits[4], (D,), jnp.float32), 0.5, 1.5),
        "ctc_weight": draw_ctc_weight(jax.random.fold_in(splits[9], 71), 0),
        "labels": draw_labels(jax.random.fold_in(splits[9], 71), 0),
        "starts": draw_starts(jax.random.fold_in(splits[9], 71), 0),
        "widths": draw_widths(jax.random.fold_in(splits[9], 71), 0),
    }


LN_EPSILON = 1e-05
NEG_SCORE = -1000000000.0

def layer_norm(values, gain_row):
    row_mean = lax.optimization_barrier(jnp.mean(values, axis=-1, keepdims=True))
    row_var = lax.optimization_barrier(jnp.mean(jnp.square(values - row_mean), axis=-1, keepdims=True))
    return (values - row_mean) * lax.rsqrt(row_var + LN_EPSILON) * gain_row

def reference(frames, up_weight, down_weight, ffn_gain, final_gain, ctc_weight, labels, starts, widths):

    def shard_emissions(shard_rows):
        normed_in = layer_norm(shard_rows.astype(jnp.float32), ffn_gain).astype(jnp.bfloat16)
        pre_act = jnp.dot(normed_in, up_weight, preferred_element_type=jnp.float32)
        hidden = jax.nn.silu(pre_act).astype(jnp.bfloat16)
        branch = jnp.dot(hidden, down_weight, preferred_element_type=jnp.float32)
        residual = shard_rows.astype(jnp.float32) + 0.5 * branch
        normed = layer_norm(residual, final_gain).astype(jnp.bfloat16)
        logits = jnp.dot(normed, ctc_weight, preferred_element_type=jnp.float32)
        return jax.nn.log_softmax(logits, axis=-1)
    per_shard = lax.map(shard_emissions, frames.reshape(SHARDS, FD, D))
    emissions = per_shard.reshape(FRAMES, V)
    band_index = jnp.arange(BAND, dtype=jnp.int32)
    window = jnp.arange(2 * BAND, dtype=jnp.int32)
    scale_out = 1.0 / FRAMES

    def shard_step(vector, shard_item):
        shard_index, shard_emit = shard_item
        prior_shard = jnp.maximum(shard_index - 1, 0)
        start_in = jnp.where(shard_index > 0, starts[prior_shard], 0).astype(jnp.int32)
        width_in = jnp.where(shard_index > 0, widths[prior_shard], 2).astype(jnp.int32)
        window_ids = lax.dynamic_slice_in_dim(labels, start_in, 2 * BAND)
        before = jnp.concatenate([jnp.full((2,), -1, jnp.int32), window_ids[:-2]])
        skip_ok = (window >= 2) & (window_ids != before)
        scores = jnp.take(shard_emit, window_ids, axis=1)
        entry_scores = jnp.where(band_index < width_in, vector, NEG_SCORE)
        path_state = jnp.concatenate([entry_scores, jnp.full((BAND,), NEG_SCORE, jnp.float32)])

        def frame_step(path_state, frame_emit):
            from_one = jnp.concatenate([jnp.full((1,), NEG_SCORE, jnp.float32), path_state[:-1]])
            from_two = jnp.concatenate([jnp.full((2,), NEG_SCORE, jnp.float32), path_state[:-2]])
            from_two = jnp.where(skip_ok, from_two, NEG_SCORE)
            return (jnp.maximum(jnp.maximum(path_state, from_one), from_two) + frame_emit, None)
        path_state, _ = lax.scan(frame_step, path_state, scores)
        offset = (starts[shard_index] - start_in).astype(jnp.int32)
        exit_scores = lax.dynamic_slice_in_dim(path_state, offset, BAND)
        live_cols = band_index < widths[shard_index]
        vector = jnp.where(live_cols, exit_scores, NEG_SCORE)
        band_row = jnp.where(live_cols, exit_scores * scale_out, 0.0)
        return (vector, band_row)
    initial = jnp.where(band_index < 2, 0.0, NEG_SCORE).astype(jnp.float32)
    _, band_scores = lax.scan(shard_step, initial, (jnp.arange(SHARDS, dtype=jnp.int32), per_shard))
    return (emissions, band_scores)
```

```python
import functools

import jax
import jax.numpy as jnp
from jax import lax
from jax.experimental import pallas as pl
from jax.experimental.pallas import tpu as pltpu
from jax.sharding import PartitionSpec as P

BAND = 128
RING = 2 * BAND
HALF = BAND // 2
LN_EPSILON = 1e-05
NEG_SCORE = -1000000000.0
CHUNKS = 1
VMEM_LIMIT = 60 * 1024 * 1024


f32 = jnp.float32
bf16 = jnp.bfloat16


def line_gather(x, n):
    r1 = lax.ppermute(x, "chan", [(i, i + 1) for i in range(n - 1)])
    l1 = lax.ppermute(x, "chan", [(i + 1, i) for i in range(n - 1)])
    r2 = []
    l2 = []
    for k in range(1, n - 1):
        r2.append(lax.ppermute(r1, "chan", [(i, i + k) for i in range(1, n - k)]))
        l2.append(lax.ppermute(l1, "chan", [(i, i - k) for i in range(k, n - 1)]))
    return [x, r1, l1, *r2, *l2]


def piece_at(a, z, n):
    if a == z:
        return 0
    if a == z - 1:
        return 1
    if a == z + 1:
        return 2
    if a < z:
        return 3 + (z - a - 1) - 1
    return 3 + (n - 2) + (a - z - 1) - 1


def line_scatter(parts, n):
    right = parts[0].astype(f32)
    left = parts[n - 2].astype(f32)
    for k in range(1, n - 1):
        got = lax.ppermute(parts[k], "chan", [(i, i + k) for i in range(0, n - 1 - k)])
        right = right + got.astype(f32)
        got = lax.ppermute(parts[n - 2 - k], "chan", [(i, i - k) for i in range(k + 1, n)])
        left = left + got.astype(f32)
    from_left = lax.ppermute(right.astype(bf16), "chan", [(i, i + 1) for i in range(n - 1)])
    from_right = lax.ppermute(left.astype(bf16), "chan", [(i + 1, i) for i in range(n - 1)])
    return from_left, from_right


def tm_gather(x, size, bits):
    dist = [0]
    for b in bits:
        got = lax.ppermute(x, "tm", [(i, i ^ (1 << b)) for i in range(size)])
        x = jnp.concatenate([x, got], axis=0)
        dist = dist + [d ^ (1 << b) for d in dist]
    got = lax.ppermute(x, "tm", [(i, i ^ 1) for i in range(size)])
    return x, got, dist


def ffn_kernel(n, dist, meta, gain, *refs):
    pieces = 1 + 2 + 2 * (n - 2)
    xs = refs[:pieces]
    ups = refs[pieces : pieces + 2]
    dns = refs[pieces + 2 : pieces + 4]
    outs = refs[pieces + 4 : pieces + 4 + n - 1]
    base = refs[pieces + 3 + n]
    xin, xn, hid, up, dn, xsem, usem, dsem = refs[pieces + 4 + n :]
    feat = xin.shape[2]
    rows = xin.shape[1]
    fc = rows // n
    width = n * feat
    up_dist, dn_dist = dist
    tall = ups[0].shape[0] // len(up_dist)
    z = meta[0]
    me = meta[1]

    for a in range(n):
        for here in range(n):

            @pl.when(z == here)
            def _(a=a, here=here):
                pltpu.make_async_copy(xs[piece_at(a, here, n)], xin.at[a], xsem.at[a]).start()

    def weight_copies(srcs, dst, sem, dist):
        made = []
        for core in range(2):
            for q, d in enumerate(dist):
                row = pl.multiple_of(lax.bitwise_xor(me, d ^ core) * tall, 16)
                made.append(
                    pltpu.make_async_copy(
                        srcs[core].at[pl.ds(q * tall, tall)],
                        dst.at[pl.ds(row, tall)],
                        sem.at[core * len(dist) + q],
                    )
                )
        return made

    up_copies = weight_copies(ups, up, usem, up_dist)
    dn_copies = weight_copies(dns, dn, dsem, dn_dist)
    for c in up_copies:
        c.start()
    for c in dn_copies:
        c.start()
    for a in range(n):
        pltpu.make_async_copy(xs[0], xin.at[a], xsem.at[a]).wait()

    for r in range(n):
        first = pl.multiple_of(lax.rem(z + r, n) * fc, fc)
        got = [xin[a, pl.ds(first, fc), :].astype(f32) for a in range(n)]
        total = got[0].sum(-1, keepdims=True)
        for a in range(1, n):
            total = total + got[a].sum(-1, keepdims=True)
        mean = total / width
        square = jnp.zeros_like(total)
        for a in range(n):
            square = square + jnp.square(got[a] - mean).sum(-1, keepdims=True)
        scale = lax.rsqrt(square / width + LN_EPSILON)
        normed = [((got[a] - mean) * scale * gain[a : a + 1, :]).astype(bf16) for a in range(n)]
        xn[r * fc : (r + 1) * fc, :] = jnp.concatenate(normed, axis=1)
        if r == 0:
            base[...] = jnp.concatenate(got, axis=1)

    for c in up_copies:
        c.wait()
    hidden = up.shape[1]
    step = min(256, hidden)
    for j in range(0, hidden, step):
        a = jnp.dot(xn[...], up[:, j : j + step], preferred_element_type=f32)
        hid[:, j : j + step] = (a / (1.0 + jnp.exp(-a))).astype(bf16)
    for c in dn_copies:
        c.wait()
    for j in range(0, width, 256):
        p = lax.dot_general(
            hid[...], dn[j : j + 256, :], (((1,), (1,)), ((), ())), preferred_element_type=f32
        )
        for r in range(1, n):
            outs[r - 1][:, j : j + 256] = p[r * fc : (r + 1) * fc].astype(bf16)
        base[:, j : j + 256] = base[:, j : j + 256] + 0.5 * p[:fc]


def ffn(meta, gain, xs, ups, dns, dist, n):
    rows, feat = xs[0].shape
    fc = rows // n
    width = n * feat
    hidden = ups[0].shape[1]
    count = 2 * len(dist[0])
    vmem = pl.BlockSpec(memory_space=pltpu.VMEM)
    anywhere = pl.BlockSpec(memory_space=pl.ANY)
    return pl.pallas_call(
        functools.partial(ffn_kernel, n, dist),
        out_shape=[jax.ShapeDtypeStruct((fc, width), bf16)] * (n - 1)
        + [jax.ShapeDtypeStruct((fc, width), f32)],
        in_specs=[pl.BlockSpec(memory_space=pltpu.SMEM), vmem] + [anywhere] * (len(xs) + 4),
        out_specs=[vmem] * n,
        scratch_shapes=[
            pltpu.VMEM((n, rows, feat), bf16),
            pltpu.VMEM((rows, width), bf16),
            pltpu.VMEM((rows, hidden), bf16),
            pltpu.VMEM((width, hidden), bf16),
            pltpu.VMEM((width, hidden), bf16),
            pltpu.SemaphoreType.DMA((n,)),
            pltpu.SemaphoreType.DMA((count,)),
            pltpu.SemaphoreType.DMA((count,)),
        ],
        compiler_params=pltpu.CompilerParams(vmem_limit_bytes=VMEM_LIMIT),
        cost_estimate=pl.CostEstimate(
            flops=4 * rows * width * hidden,
            bytes_accessed=4 * width * hidden + 6 * rows * width,
            transcendentals=rows * hidden,
        ),
        name="ffn",
    )(meta, gain, *xs, *ups, *dns)


def band_states(shard, starts, widths):
    prior = jnp.maximum(shard - 1, 0)
    start_in = jnp.where(shard > 0, starts[prior], 0)
    width_in = jnp.where(shard > 0, widths[prior], 2)
    return start_in, width_in, starts[shard], widths[shard]


def ring_states(start_in, odd, shape):
    lane = lax.broadcasted_iota(jnp.int32, shape, len(shape) - 1)
    state = 2 * lane + odd + (start_in // RING) * RING
    return jnp.where(state >= start_in, state, state + RING)


def tail_kernel(first, last, meta, starts, widths, base, left, right, gain, ctc, label_rows, *refs):
    if not first:
        state_in, refs = refs[0], refs[1:]
    emit, state_out, gaps = refs
    start_in, width_in, start_out, width_out = band_states(meta[2], starts, widths)

    residual = base[...] + 0.5 * (left[...].astype(f32) + right[...].astype(f32))
    mean = jnp.mean(residual, axis=-1, keepdims=True)
    var = jnp.mean(jnp.square(residual - mean), axis=-1, keepdims=True)
    normed = ((residual - mean) * lax.rsqrt(var + LN_EPSILON) * gain[...]).astype(bf16)
    logits = jnp.dot(normed, ctc[...], preferred_element_type=f32)
    logits = logits - jnp.max(logits, axis=-1, keepdims=True)
    emissions = logits - jnp.log(jnp.sum(jnp.exp(logits), axis=-1, keepdims=True))
    emit[...] = emissions

    state_a = ring_states(start_in, 0, (8, BAND))
    state_b = ring_states(start_in, 1, (8, BAND))
    row = start_in // RING
    after = jnp.minimum(row + 1, label_rows.shape[0] - 1)
    ids = jnp.where(
        state_b // RING == row,
        jnp.broadcast_to(label_rows[pl.ds(row, 1), :], (8, BAND)),
        jnp.broadcast_to(label_rows[pl.ds(after, 1), :], (8, BAND)),
    )
    skip = (state_b - start_in >= 2) & (ids != pltpu.roll(ids, 1, axis=1))
    no_a = state_a == start_in
    no_b = state_b == start_in

    vocab = emissions.shape[1]
    chosen = lax.broadcasted_iota(jnp.int32, (vocab, BAND), 0) == jnp.broadcast_to(
        ids[0:1], (vocab, BAND)
    )
    choose = chosen.astype(f32).astype(bf16)
    rest = emissions
    picked = jnp.zeros((emissions.shape[0], BAND), f32)
    for _ in range(3):
        part = rest.astype(bf16)
        rest = rest - part.astype(f32)
        picked = picked + jnp.dot(part, choose, preferred_element_type=f32)
    blank = emissions[:, 0:1]
    gaps[...] = picked - blank
    blank_total = jnp.sum(blank)

    groups = BAND // 8
    lane = lax.broadcasted_iota(jnp.int32, (8, BAND), 1)
    sub = lax.broadcasted_iota(jnp.int32, (8, BAND), 0)
    if first:
        slot = jnp.where(lane < HALF, lane, lane - HALF)
        live_a = state_a - start_in < width_in
        live_b = state_b - start_in < width_in
        a_rows = [
            jnp.where((slot == sub + 8 * g) & live_a, 0.0, NEG_SCORE) for g in range(groups)
        ]
        b_rows = [
            jnp.where((slot + HALF == sub + 8 * g) & live_b, 0.0, NEG_SCORE) for g in range(groups)
        ]
    else:
        a_rows = [state_in[0, 8 * g : 8 * g + 8, :] for g in range(groups)]
        b_rows = [state_in[1, 8 * g : 8 * g + 8, :] for g in range(groups)]

    def steps(t, carry):
        a_rows, b_rows = [list(v) for v in carry]
        tile = gaps[pl.ds(pl.multiple_of(t * 8, 8), 8), :]
        for u in range(8):
            gap = jnp.broadcast_to(tile[u : u + 1], (8, BAND))
            for g in range(groups):
                a, b = a_rows[g], b_rows[g]
                back = pltpu.roll(b, 1, axis=1)
                new_a = jnp.maximum(a, jnp.where(no_a, NEG_SCORE, back))
                come = jnp.where(no_b, NEG_SCORE, jnp.where(skip, new_a, a))
                a_rows[g] = new_a
                b_rows[g] = jnp.maximum(b, come) + gap
        return tuple(a_rows), tuple(b_rows)

    a_rows, b_rows = lax.fori_loop(
        0, emissions.shape[0] // 8, steps, (tuple(a_rows), tuple(b_rows))
    )
    if last:
        out_a = (state_a >= start_out) & (state_a < start_out + width_out)
        out_b = (state_b >= start_out) & (state_b < start_out + width_out)
        for g in range(groups):
            a = jnp.where(out_a, a_rows[g], NEG_SCORE)
            b = jnp.where(out_b, b_rows[g], NEG_SCORE)
            a = jnp.maximum(a, pltpu.roll(a, HALF, axis=1))
            b = jnp.maximum(b, pltpu.roll(b, HALF, axis=1))
            state_out[8 * g : 8 * g + 8, :] = jnp.where(lane < HALF, a, b) + blank_total
    else:
        for g in range(groups):
            state_out[0, 8 * g : 8 * g + 8, :] = a_rows[g] + blank_total
            state_out[1, 8 * g : 8 * g + 8, :] = b_rows[g] + blank_total


def tail(first, last, meta, starts, widths, base, left, right, gain, ctc, label_rows, *state):
    fc = base.shape[0]
    vocab = ctc.shape[1]
    smem = pl.BlockSpec(memory_space=pltpu.SMEM)
    vmem = pl.BlockSpec(memory_space=pltpu.VMEM)
    shape = (BAND, BAND) if last else (2, BAND, BAND)
    return pl.pallas_call(
        functools.partial(tail_kernel, first, last),
        out_shape=[jax.ShapeDtypeStruct((fc, vocab), f32), jax.ShapeDtypeStruct(shape, f32)],
        in_specs=[smem] * 3 + [vmem] * (6 + len(state)),
        out_specs=[vmem] * 2,
        scratch_shapes=[pltpu.VMEM((fc, BAND), f32)],
        compiler_params=pltpu.CompilerParams(vmem_limit_bytes=VMEM_LIMIT),
        cost_estimate=pl.CostEstimate(
            flops=40 * fc * BAND * BAND, bytes_accessed=16 * fc * gain.shape[1], transcendentals=fc * vocab
        ),
        name="tail",
    )(meta, starts, widths, base, left, right, gain, ctc, label_rows, *state)


def product_kernel(mats, out, left):
    groups = BAND // 8
    out[...] = mats[0]

    def lap(k, _):
        left[...] = out[...]

        def block(j, acc):
            shift = lax.rem(BAND - 8 * j, BAND)
            terms = [
                pltpu.roll(left[8 * g : 8 * g + 8, :], shift, axis=1) for g in range(groups)
            ]
            later = mats[k, pl.ds(pl.multiple_of(8 * j, 8), 8), :]
            acc = list(acc)
            for u in range(8):
                row = jnp.broadcast_to(later[u : u + 1], (8, BAND))
                for g in range(groups):
                    col = jnp.broadcast_to(terms[g][:, u : u + 1], (8, BAND))
                    acc[g] = jnp.maximum(acc[g], col + row)
            return tuple(acc)

        none = jnp.full((8, BAND), 64 * NEG_SCORE, f32)
        acc = lax.fori_loop(0, BAND // 8, block, (none,) * groups)
        for g in range(groups):
            out[8 * g : 8 * g + 8, :] = acc[g]
        return 0

    lax.fori_loop(1, mats.shape[0], lap, 0)


def product(mats):
    vmem = pl.BlockSpec(memory_space=pltpu.VMEM)
    return pl.pallas_call(
        product_kernel,
        out_shape=jax.ShapeDtypeStruct((BAND, BAND), f32),
        in_specs=[vmem],
        out_specs=vmem,
        scratch_shapes=[pltpu.VMEM((BAND, BAND), f32)],
        compiler_params=pltpu.CompilerParams(vmem_limit_bytes=VMEM_LIMIT),
        name="product",
    )(mats)


def score_kernel(scale, meta, starts, widths, near, far, out):
    z = meta[0]
    me = meta[1]
    start_in, width_in, start_out, width_out = band_states(meta[2], starts, widths)
    sub = lax.broadcasted_iota(jnp.int32, (BAND, BAND), 0)
    lane = lax.broadcasted_iota(jnp.int32, (BAND, BAND), 1)

    def through(col, mat):
        return jnp.max(col + mat, axis=0, keepdims=True)

    def turn(row):
        return jnp.max(
            jnp.where(sub == lane, jnp.broadcast_to(row, (BAND, BAND)), 64 * NEG_SCORE),
            axis=1,
            keepdims=True,
        )

    place = lax.broadcasted_iota(jnp.int32, (BAND, 1), 0)
    col = jnp.where((place == 0) | (place == HALF), 0.0, NEG_SCORE).astype(f32)
    col = lax.fori_loop(0, me, lambda g, c: turn(through(c, far[g])), col)
    col = lax.fori_loop(0, z, lambda k, c: turn(through(c, near[k])), col)
    col = turn(through(col, near[z]))
    state = start_out + lane
    left = lax.rem(state, BAND)
    home = left // 2 + HALF * lax.rem(left, 2)
    best = jnp.max(jnp.where(sub == home, col, 64 * NEG_SCORE), axis=0, keepdims=True)
    live = lax.broadcasted_iota(jnp.int32, (1, BAND), 1) < width_out
    out[...] = jnp.where(live, best * scale, 0.0)


def scores(scale, meta, starts, widths, near, far):
    smem = pl.BlockSpec(memory_space=pltpu.SMEM)
    vmem = pl.BlockSpec(memory_space=pltpu.VMEM)
    return pl.pallas_call(
        functools.partial(score_kernel, scale),
        out_shape=jax.ShapeDtypeStruct((1, BAND), f32),
        in_specs=[smem] * 3 + [vmem] * 2,
        out_specs=vmem,
        compiler_params=pltpu.CompilerParams(vmem_limit_bytes=VMEM_LIMIT),
        name="scores",
    )(meta, starts, widths, near, far)


def local(frames, up_weight, down_weight, ffn_gain, final_gain, ctc_weight, labels, starts, widths):
    n = lax.axis_size("chan")
    z = lax.axis_index("chan")
    size = lax.axis_size("tm")
    me = lax.axis_index("tm")
    rows, feat = frames.shape
    fd = rows // n
    fc = fd // CHUNKS
    shard = me * n + z
    meta = jnp.stack([z, me, shard]).astype(jnp.int32)
    high = list(range(1, size.bit_length() - 1))
    label_rows = labels.reshape(-1, BAND, 2)[:, :, 1]

    blocks = frames.reshape(n, CHUNKS, fc, feat)
    gathered = [line_gather(blocks[:, c].reshape(n * fc, feat), n) for c in range(CHUNKS)]
    up_own, up_other, dist = tm_gather(up_weight, size, high)
    dn_own, dn_other, dn_dist = tm_gather(down_weight.T, size, high[::-1])

    gain = ffn_gain.reshape(n, feat)
    state = ()
    emitted = []
    for c in range(CHUNKS):
        *parts, base = ffn(
            meta, gain, gathered[c], (up_own, up_other), (dn_own, dn_other), (dist, dn_dist), n
        )
        from_left, from_right = line_scatter(parts, n)
        emissions, state = tail(
            c == 0,
            c == CHUNKS - 1,
            meta,
            starts,
            widths,
            base,
            from_left,
            from_right,
            final_gain.reshape(1, -1),
            ctc_weight,
            label_rows,
            *((state,) if c else ()),
        )
        emitted.append(emissions)
    emissions = jnp.concatenate(emitted, axis=0) if CHUNKS > 1 else emitted[0]

    near = lax.all_gather(state, "chan")
    far = lax.all_gather(product(near), "tm")
    band_row = scores(1.0 / (rows * size), meta, starts, widths, near, far)
    return emissions, band_row


def solution(mesh):
    in_specs = (P("tm", "chan"), P("tm", "chan"), P("chan", "tm"), P(), P(), P(), P(), P(), P())
    out_specs = (P(("tm", "chan"), None), P(("tm", "chan"), None))
    return jax.shard_map(local, mesh=mesh, in_specs=in_specs, out_specs=out_specs, check_vma=False)
```

```python
import functools

import jax
import jax.numpy as jnp
from jax import lax
from jax.experimental import pallas as pl
from jax.experimental.pallas import tpu as pltpu
from jax.sharding import PartitionSpec as P


BAND = 128
RING = 2 * BAND
LANES = 128
PHASES = 8
LANE_STATES = RING // PHASES
LANE_ROWS = LANES // LANE_STATES
LN_EPSILON = 1e-05
NEG_SCORE = -1000000000.0
CHUNKS = 2
VMEM_LIMIT = 24 * 1024 * 1024
FFN_VMEM = 40 * 1024 * 1024


f32 = jnp.float32
bf16 = jnp.bfloat16


def line_gather(x, n):
    r1 = lax.ppermute(x, "chan", [(i, i + 1) for i in range(n - 1)])
    l1 = lax.ppermute(x, "chan", [(i + 1, i) for i in range(n - 1)])
    r2 = []
    l2 = []
    for k in range(1, n - 1):
        r2.append(lax.ppermute(r1, "chan", [(i, i + k) for i in range(1, n - k)]))
        l2.append(lax.ppermute(l1, "chan", [(i, i - k) for i in range(k, n - 1)]))
    return [x, r1, l1, *r2, *l2]


def piece_at(a, z, n):
    if a == z:
        return 0
    if a == z - 1:
        return 1
    if a == z + 1:
        return 2
    if a < z:
        return 3 + (z - a - 1) - 1
    return 3 + (n - 2) + (a - z - 1) - 1


def line_scatter(parts, n):
    right = parts[0].astype(f32)
    left = parts[n - 2].astype(f32)
    for k in range(1, n - 1):
        got = lax.ppermute(parts[k], "chan", [(i, i + k) for i in range(0, n - 1 - k)])
        right = right + got.astype(f32)
        got = lax.ppermute(parts[n - 2 - k], "chan", [(i, i - k) for i in range(k + 1, n)])
        left = left + got.astype(f32)
    from_left = lax.ppermute(right.astype(bf16), "chan", [(i, i + 1) for i in range(n - 1)])
    from_right = lax.ppermute(left.astype(bf16), "chan", [(i + 1, i) for i in range(n - 1)])
    return from_left, from_right


def tm_gather(x, size, bits):
    dist = [0]
    for b in bits:
        got = lax.ppermute(x, "tm", [(i, i ^ (1 << b)) for i in range(size)])
        x = jnp.concatenate([x, got], axis=0)
        dist = dist + [d ^ (1 << b) for d in dist]
    got = lax.ppermute(x, "tm", [(i, i ^ 1) for i in range(size)])
    return x, got, dist


def prepare_kernel(dist, meta, *refs):
    ups, dns = refs[0:2], refs[2:4]
    up_t, dn_t, up, usem, dsem = refs[4:]
    up_dist, dn_dist = dist
    tall = ups[0].shape[0] // len(up_dist)
    me = meta[1]

    def copies(srcs, dst, sem, dist):
        made = []
        for core in range(2):
            for q, d in enumerate(dist):
                row = pl.multiple_of(lax.bitwise_xor(me, d ^ core) * tall, 16)
                made.append(
                    pltpu.make_async_copy(
                        srcs[core].at[pl.ds(q * tall, tall)],
                        dst.at[pl.ds(row, tall)],
                        sem.at[core * len(dist) + q],
                    )
                )
        return made

    up_copies = copies(ups, up, usem, up_dist)
    dn_copies = copies(dns, dn_t, dsem, dn_dist)
    for c in up_copies + dn_copies:
        c.start()
    for c in up_copies:
        c.wait()
    step = 256
    for i in range(0, up.shape[0], step):
        for j in range(0, up.shape[1], step):
            wide = min(step, up.shape[1] - j)
            up_t[j : j + wide, i : i + step] = up[i : i + step, j : j + wide].T
    for c in dn_copies:
        c.wait()


def prepare(meta, ups, dns, dist, width):
    hidden = ups[0].shape[1]
    count = 2 * len(dist[0])
    vmem = pl.BlockSpec(memory_space=pltpu.VMEM)
    anywhere = pl.BlockSpec(memory_space=pl.ANY)
    return pl.pallas_call(
        functools.partial(prepare_kernel, dist),
        out_shape=[
            jax.ShapeDtypeStruct((hidden, width), bf16),
            jax.ShapeDtypeStruct((width, hidden), bf16),
        ],
        in_specs=[pl.BlockSpec(memory_space=pltpu.SMEM)] + [anywhere] * 4,
        out_specs=[vmem] * 2,
        scratch_shapes=[
            pltpu.VMEM((width, hidden), bf16),
            pltpu.SemaphoreType.DMA((count,)),
            pltpu.SemaphoreType.DMA((count,)),
        ],
        compiler_params=pltpu.CompilerParams(vmem_limit_bytes=VMEM_LIMIT),
        cost_estimate=pl.CostEstimate(
            flops=0, bytes_accessed=8 * width * hidden, transcendentals=0
        ),
        name="prepare",
    )(meta, *ups, *dns)


def ffn_kernel(n, chunk, chunks, meta, gain, up_hbm, dn_hbm, *refs):
    pieces = 1 + 2 + 2 * (n - 2)
    xs = refs[:pieces]
    outs = refs[pieces : pieces + n]
    xin, xn, hid, up_t, dn_t, terms, base, xsem, wsem, osem = refs[pieces + n :]
    width, rows = xin.shape
    feat = width // n
    fc = rows // n
    z = meta[0]
    for a in range(n):
        for here in range(n):

            @pl.when(z == here)
            def _(a=a, here=here):
                for r in range(n):
                    column = (((here + r) % n) * chunks + chunk) * fc
                    pltpu.make_async_copy(
                        xs[piece_at(a, here, n)].at[:, pl.ds(column, fc)],
                        xin.at[pl.ds(a * feat, feat), pl.ds(r * fc, fc)],
                        xsem.at[a * n + r],
                    ).start()

    up_copy = pltpu.make_async_copy(up_hbm, up_t, wsem.at[0])
    dn_copy = pltpu.make_async_copy(dn_hbm, dn_t, wsem.at[1])
    up_copy.start()
    dn_copy.start()

    for r in range(n):
        for a in range(n):
            pltpu.make_async_copy(
                xs[0].at[:, pl.ds(0, fc)],
                xin.at[pl.ds(a * feat, feat), pl.ds(r * fc, fc)],
                xsem.at[a * n + r],
            ).wait()
    up_copy.wait()
    hidden = up_t.shape[0]
    step = 256 if hidden % 256 == 0 else 128
    half = max(rows // 2, 256)
    for start in range(0, rows, half):
        for h in range(start, start + half, 128):
            x = xin[:, h : h + 128].astype(f32)
            mean = jnp.mean(x, axis=0, keepdims=True)
            var = jnp.mean(jnp.square(x - mean), axis=0, keepdims=True)
            normed = (x - mean) * lax.rsqrt(var + LN_EPSILON) * gain[...]
            xn[:, h : h + 128] = normed.astype(bf16)
        for j in range(0, hidden, step):
            a = jnp.dot(
                up_t[j : j + step, :], xn[:, start : start + half], preferred_element_type=f32
            )
            hid[j : j + step, start : start + half] = (a / (1.0 + jnp.exp(-a))).astype(bf16)
    dn_copy.wait()
    copies = []
    for k, j in enumerate(range(0, width, 256)):
        p = jnp.dot(dn_t[j : j + 256, :], hid[...], preferred_element_type=f32)
        for r in range(n):
            term = p[:, r * fc : (r + 1) * fc]
            if r == 0:
                base[j : j + 256, :] = xin[j : j + 256, :fc].astype(f32) + 0.5 * term
                src = base.at[pl.ds(j, 256)]
            else:
                terms[r - 1, j : j + 256, :] = term.astype(bf16)
                src = terms.at[r - 1, pl.ds(j, 256)]
            copy = pltpu.make_async_copy(
                src, outs[(r - 1) % n].at[pl.ds(j, 256)], osem.at[k * n + r]
            )
            copy.start()
            copies.append(copy)
    for copy in copies:
        copy.wait()


def ffn(meta, gain, up_t, dn_t, xs, n, chunk, chunks):
    _, rows = xs[0].shape
    rows = rows // chunks
    fc = rows // n
    hidden, width = up_t.shape
    vmem = pl.BlockSpec(memory_space=pltpu.VMEM)
    anywhere = pl.BlockSpec(memory_space=pl.ANY)
    return pl.pallas_call(
        functools.partial(ffn_kernel, n, chunk, chunks),
        out_shape=[jax.ShapeDtypeStruct((width, fc), bf16)] * (n - 1)
        + [jax.ShapeDtypeStruct((width, fc), f32)],
        in_specs=[pl.BlockSpec(memory_space=pltpu.SMEM), vmem] + [anywhere] * (2 + len(xs)),
        out_specs=[anywhere] * n,
        scratch_shapes=[
            pltpu.VMEM((width, rows), bf16),
            pltpu.VMEM((width, rows), bf16),
            pltpu.VMEM((hidden, rows), bf16),
            pltpu.VMEM((hidden, width), bf16),
            pltpu.VMEM((width, hidden), bf16),
            pltpu.VMEM((n - 1, width, fc), bf16),
            pltpu.VMEM((width, fc), f32),
            pltpu.SemaphoreType.DMA((n * n,)),
            pltpu.SemaphoreType.DMA((2,)),
            pltpu.SemaphoreType.DMA((n * (width // 256),)),
        ],
        compiler_params=pltpu.CompilerParams(vmem_limit_bytes=FFN_VMEM),
        cost_estimate=pl.CostEstimate(
            flops=4 * rows * width * hidden,
            bytes_accessed=4 * width * hidden + 6 * rows * width,
            transcendentals=rows * hidden,
        ),
        name="ffn",
    )(meta, gain, up_t, dn_t, *xs)


def band_states(shard, starts, widths):
    prior = jnp.maximum(shard - 1, 0)
    start_in = jnp.where(shard > 0, starts[prior], 0)
    width_in = jnp.where(shard > 0, widths[prior], 2)
    return start_in, width_in, starts[shard], widths[shard]


def tail_kernel(first, last, meta, starts, widths, base, left, right, gain, ctc_t, label_rows, *refs):
    if not first:
        state_in, refs = refs[0], refs[1:]
    emit, state_out, gaps = refs
    start_in, width_in, start_out, width_out = band_states(meta[2], starts, widths)

    residual = base[...] + 0.5 * (left[...].astype(f32) + right[...].astype(f32))
    mean = jnp.mean(residual, axis=0, keepdims=True)
    var = jnp.mean(jnp.square(residual - mean), axis=0, keepdims=True)
    normed = ((residual - mean) * lax.rsqrt(var + LN_EPSILON) * gain[...]).astype(bf16)
    logits = jnp.dot(ctc_t[...], normed, preferred_element_type=f32)
    logits = logits - jnp.max(logits, axis=0, keepdims=True)
    emissions = (logits - jnp.log(jnp.sum(jnp.exp(logits), axis=0, keepdims=True))).T
    emit[...] = emissions

    odd_start = lax.rem(start_in, 2)
    origin = start_in - odd_start
    row = start_in // RING
    after = jnp.minimum(row + 1, label_rows.shape[0] - 1)
    ring = row * RING + lax.broadcasted_iota(jnp.int32, (8, RING), 1)
    around = jnp.where(
        ring >= start_in,
        jnp.broadcast_to(label_rows[pl.ds(row, 1), :], (8, RING)),
        jnp.broadcast_to(label_rows[pl.ds(after, 1), :], (8, RING)),
    )
    lane = lax.broadcasted_iota(jnp.int32, (8, LANES), 1)
    sub = lax.broadcasted_iota(jnp.int32, (8, LANES), 0)
    spot = lax.rem(lane, LANE_STATES)
    block = lane // LANE_STATES
    odd_phases = list(range(1, PHASES, 2))

    shape = (RING, LANES * len(odd_phases))
    held = lax.broadcasted_iota(jnp.int32, shape, 1)
    held = origin + PHASES * lax.rem(held, LANE_STATES) + 2 * (held // LANES) + 1
    pick = lax.broadcasted_iota(jnp.int32, shape, 0) == lax.rem(held, RING)
    ids = jnp.dot(
        around.astype(f32).astype(bf16), pick.astype(f32).astype(bf16), preferred_element_type=f32
    ).astype(jnp.int32)
    ids_of = {p: ids[:, LANES * k : LANES * (k + 1)] for k, p in enumerate(odd_phases)}
    skip = {}
    for p in odd_phases:
        if p == 1:
            behind = pltpu.roll(ids_of[PHASES - 1], 1, axis=1)
        else:
            behind = ids_of[p - 2]
        skip[p] = (PHASES * spot + p - odd_start >= 2) & (ids_of[p] != behind)
    no_back = (spot == 0) & (odd_start == 0)
    no_rise = (spot == 0) & (odd_start == 1)

    vocab = emissions.shape[1]
    choose = (
        lax.broadcasted_iota(jnp.int32, (vocab, shape[1]), 0)
        == jnp.broadcast_to(ids[0:1], (vocab, shape[1]))
    )
    choose = choose.astype(f32).astype(bf16)
    rest = emissions
    picked = jnp.zeros((emissions.shape[0], shape[1]), f32)
    for _ in range(3):
        part = rest.astype(bf16)
        rest = rest - part.astype(f32)
        picked = picked + jnp.dot(part, choose, preferred_element_type=f32)
    blank = emissions[:, 0:1]
    gaps[...] = picked - blank
    blank_total = jnp.sum(blank)

    groups = BAND // (8 * LANE_ROWS)
    if first:
        rows = []
        for g in range(groups):
            entry = g * 8 * LANE_ROWS + 8 * block + sub
            for p in range(PHASES):
                state = origin + PHASES * spot + p
                live = (state >= start_in) & (state < start_in + jnp.minimum(width_in, BAND))
                rows.append(jnp.where(live & (lax.rem(state, BAND) == entry), 0.0, NEG_SCORE))
    else:
        rows = [state_in[k] for k in range(groups * PHASES)]

    def steps(t, rows):
        rows = list(rows)
        start = pl.multiple_of(t * 8, 8)
        tiles = {
            p: gaps[pl.ds(start, 8), LANES * k : LANES * (k + 1)] for k, p in enumerate(odd_phases)
        }
        for u in range(8):
            gap = {p: jnp.broadcast_to(tiles[p][u : u + 1], (8, LANES)) for p in odd_phases}
            for g in range(groups):
                was = rows[g * PHASES : (g + 1) * PHASES]
                now = list(was)
                back = jnp.where(no_back, NEG_SCORE, pltpu.roll(was[PHASES - 1], 1, axis=1))
                for p in range(0, PHASES, 2):
                    now[p] = jnp.maximum(was[p], back if p == 0 else was[p - 1])
                for p in odd_phases:
                    come = jnp.where(skip[p], now[p - 1], was[p - 1])
                    if p == 1:
                        come = jnp.where(no_rise, NEG_SCORE, come)
                    now[p] = jnp.maximum(was[p], come) + gap[p]
                rows[g * PHASES : (g + 1) * PHASES] = now
        return tuple(rows)

    rows = lax.fori_loop(0, emissions.shape[0] // 8, steps, tuple(rows))
    if not last:
        for k in range(groups * PHASES):
            state_out[k] = rows[k] + blank_total
        return

    stack = jnp.concatenate(
        [
            jnp.concatenate([rows[g * PHASES + p] for p in range(PHASES)], axis=1)
            for g in range(groups)
        ],
        axis=0,
    )
    parts = []
    for _ in range(3):
        part = stack.astype(bf16)
        stack = stack - part.astype(f32)
        parts.append(part.astype(f32))
    parts = jnp.concatenate(parts, axis=0).astype(bf16)
    count = groups * 8
    where = lax.broadcasted_iota(jnp.int32, (PHASES * LANES, 1), 0)
    slot = lax.rem(where, LANES)
    state = origin + PHASES * lax.rem(slot, LANE_STATES) + where // LANES
    owner = slot // LANE_STATES
    beyond = (state == origin) & (odd_start == 1)
    state = jnp.where(beyond, origin + RING, state)
    owner = jnp.where(beyond, lax.rem(owner + LANE_ROWS - 1, LANE_ROWS), owner)
    leaves = (state >= start_out) & (state < start_out + BAND)
    column = jnp.where(leaves, lax.rem(state, BAND), -1)
    wanted = lax.broadcasted_iota(jnp.int32, (PHASES * LANES, BAND), 1)
    exit_residue = lax.broadcasted_iota(jnp.int32, (8, BAND), 1)
    ahead = lax.rem(exit_residue - lax.rem(start_out, BAND) + BAND, BAND)
    for e in range(LANE_ROWS):
        take = jnp.where(owner == e, column, -1) == wanted
        got = jnp.dot(parts, take.astype(f32).astype(bf16), preferred_element_type=f32)
        got = got[:count] + got[count : 2 * count] + got[2 * count :]
        for g in range(groups):
            first_row = g * 8 * LANE_ROWS + 8 * e
            state_out[first_row : first_row + 8, :] = jnp.where(
                ahead < width_out, got[8 * g : 8 * g + 8] + blank_total, NEG_SCORE
            )


def tail(first, last, meta, starts, widths, base, left, right, gain, ctc_t, label_rows, *state):
    fc = base.shape[1]
    vocab = ctc_t.shape[0]
    smem = pl.BlockSpec(memory_space=pltpu.SMEM)
    vmem = pl.BlockSpec(memory_space=pltpu.VMEM)
    shape = (BAND, BAND) if last else (RING * BAND // (8 * LANES), 8, LANES)
    return pl.pallas_call(
        functools.partial(tail_kernel, first, last),
        out_shape=[jax.ShapeDtypeStruct((fc, vocab), f32), jax.ShapeDtypeStruct(shape, f32)],
        in_specs=[smem] * 3 + [vmem] * (6 + len(state)),
        out_specs=[vmem] * 2,
        scratch_shapes=[pltpu.VMEM((fc, LANES * PHASES // 2), f32)],
        compiler_params=pltpu.CompilerParams(vmem_limit_bytes=VMEM_LIMIT),
        cost_estimate=pl.CostEstimate(
            flops=40 * fc * BAND * BAND, bytes_accessed=16 * fc * gain.shape[0], transcendentals=fc * vocab
        ),
        name="tail",
    )(meta, starts, widths, base, left, right, gain, ctc_t, label_rows, *state)


def product_kernel(mats, out, left):
    groups = BAND // 8
    out[...] = mats[0]

    def lap(k, _):
        left[...] = out[...]

        def block(j, acc):
            shift = lax.rem(BAND - 8 * j, BAND)
            terms = [
                pltpu.roll(left[8 * g : 8 * g + 8, :], shift, axis=1) for g in range(groups)
            ]
            later = mats[k, pl.ds(pl.multiple_of(8 * j, 8), 8), :]
            acc = list(acc)
            for u in range(8):
                row = jnp.broadcast_to(later[u : u + 1], (8, BAND))
                for g in range(groups):
                    col = jnp.broadcast_to(terms[g][:, u : u + 1], (8, BAND))
                    acc[g] = jnp.maximum(acc[g], col + row)
            return tuple(acc)

        none = jnp.full((8, BAND), 64 * NEG_SCORE, f32)
        acc = lax.fori_loop(0, BAND // 8, block, (none,) * groups)
        for g in range(groups):
            out[8 * g : 8 * g + 8, :] = acc[g]
        return 0

    lax.fori_loop(1, mats.shape[0], lap, 0)


def product(mats):
    vmem = pl.BlockSpec(memory_space=pltpu.VMEM)
    return pl.pallas_call(
        product_kernel,
        out_shape=jax.ShapeDtypeStruct((BAND, BAND), f32),
        in_specs=[vmem],
        out_specs=vmem,
        scratch_shapes=[pltpu.VMEM((BAND, BAND), f32)],
        compiler_params=pltpu.CompilerParams(vmem_limit_bytes=VMEM_LIMIT),
        name="product",
    )(mats)


def score_kernel(scale, meta, starts, widths, near, far, out):
    z = meta[0]
    me = meta[1]
    _, _, start_out, width_out = band_states(meta[2], starts, widths)
    sub = lax.broadcasted_iota(jnp.int32, (BAND, BAND), 0)
    lane = lax.broadcasted_iota(jnp.int32, (BAND, BAND), 1)

    def through(col, mat):
        return jnp.max(col + mat, axis=0, keepdims=True)

    def turn(row):
        return jnp.max(
            jnp.where(sub == lane, jnp.broadcast_to(row, (BAND, BAND)), 64 * NEG_SCORE),
            axis=1,
            keepdims=True,
        )

    place = lax.broadcasted_iota(jnp.int32, (BAND, 1), 0)
    col = jnp.where(place < 2, 0.0, NEG_SCORE).astype(f32)
    col = lax.fori_loop(0, me, lambda g, c: turn(through(c, far[g])), col)
    col = lax.fori_loop(0, z, lambda k, c: turn(through(c, near[k])), col)
    col = turn(through(col, near[z]))
    home = lax.rem(start_out + lane, BAND)
    best = jnp.max(jnp.where(sub == home, col, 64 * NEG_SCORE), axis=0, keepdims=True)
    live = lax.broadcasted_iota(jnp.int32, (1, BAND), 1) < width_out
    out[...] = jnp.where(live, best * scale, 0.0)


def scores(scale, meta, starts, widths, near, far):
    smem = pl.BlockSpec(memory_space=pltpu.SMEM)
    vmem = pl.BlockSpec(memory_space=pltpu.VMEM)
    return pl.pallas_call(
        functools.partial(score_kernel, scale),
        out_shape=jax.ShapeDtypeStruct((1, BAND), f32),
        in_specs=[smem] * 3 + [vmem] * 2,
        out_specs=vmem,
        compiler_params=pltpu.CompilerParams(vmem_limit_bytes=VMEM_LIMIT),
        name="scores",
    )(meta, starts, widths, near, far)


def compute(frames, up_weight, down_weight, ffn_gain, final_gain, ctc_weight, labels, starts, widths):
    n = lax.axis_size("chan")
    z = lax.axis_index("chan")
    size = lax.axis_size("tm")
    me = lax.axis_index("tm")
    rows, feat = frames.shape
    shard = me * n + z
    meta = jnp.stack([z, me, shard]).astype(jnp.int32)
    high = list(range(1, size.bit_length() - 1))
    label_rows = labels.reshape(-1, RING)
    gain = ffn_gain.reshape(-1, 1)
    last_gain = final_gain.reshape(-1, 1)
    ctc_t = ctc_weight.T

    gathered = line_gather(frames.T, n)
    up_own, up_other, dist = tm_gather(up_weight, size, high)
    dn_own, dn_other, dn_dist = tm_gather(down_weight.T, size, high[::-1])
    up_t, dn_t = prepare(
        meta, (up_own, up_other), (dn_own, dn_other), (dist, dn_dist), n * feat
    )

    state = ()
    emitted = []
    for c in range(CHUNKS):
        *parts, base = ffn(meta, gain, up_t, dn_t, gathered, n, c, CHUNKS)
        from_left, from_right = line_scatter(parts, n)
        emissions, state = tail(
            c == 0,
            c == CHUNKS - 1,
            meta,
            starts,
            widths,
            base,
            from_left,
            from_right,
            last_gain,
            ctc_t,
            label_rows,
            *((state,) if c else ()),
        )
        emitted.append(emissions)
    emissions = jnp.concatenate(emitted, axis=0) if CHUNKS > 1 else emitted[0]

    near = lax.all_gather(state, "chan")
    far = lax.all_gather(product(near), "tm")
    band_row = scores(1.0 / (rows * size), meta, starts, widths, near, far)
    return emissions, band_row


def solution(mesh):
    in_specs = (P("tm", "chan"), P("tm", "chan"), P("chan", "tm"), P(), P(), P(), P(), P(), P())
    out_specs = (P(("tm", "chan"), None), P(("tm", "chan"), None))
    return jax.shard_map(compute, mesh=mesh, in_specs=in_specs, out_specs=out_specs, check_vma=False)
```

```python
import functools

import jax
import jax.numpy as jnp
from jax import lax
from jax.experimental import pallas as pl
from jax.experimental.pallas import tpu as pltpu
from jax.sharding import PartitionSpec as P


BAND = 128
RING = 2 * BAND
LANES = 128
PHASES = 8
LANE_STATES = RING // PHASES
LANE_ROWS = LANES // LANE_STATES
LN_EPSILON = 1e-05
NEG_SCORE = -1000000000.0
CHUNKS = 2
VMEM_LIMIT = 24 * 1024 * 1024
FFN_VMEM = 28 * 1024 * 1024


f32 = jnp.float32
bf16 = jnp.bfloat16


def turn_gather(x, n):
    got = [x]
    for k in range(1, n):
        got.append(lax.ppermute(x, "chan", [(i, (i + k) % n) for i in range(n)]))
    return got


def line_gather(x, n):
    r1 = lax.ppermute(x, "chan", [(i, i + 1) for i in range(n - 1)])
    l1 = lax.ppermute(x, "chan", [(i + 1, i) for i in range(n - 1)])
    r2 = []
    l2 = []
    for k in range(1, n - 1):
        r2.append(lax.ppermute(r1, "chan", [(i, i + k) for i in range(1, n - k)]))
        l2.append(lax.ppermute(l1, "chan", [(i, i - k) for i in range(k, n - 1)]))
    return [x, r1, l1, *r2, *l2]


def piece_at(a, z, n, straight):
    if straight:
        return (z - a) % n
    if a == z:
        return 0
    if a == z - 1:
        return 1
    if a == z + 1:
        return 2
    if a < z:
        return 3 + (z - a - 1) - 1
    return 3 + (n - 2) + (a - z - 1) - 1


def line_scatter(parts, n):
    right = parts[0].astype(f32)
    left = parts[n - 2].astype(f32)
    for k in range(1, n - 1):
        to_right = lax.ppermute(parts[k], "chan", [(i, i + k) for i in range(0, n - 1 - k)])
        to_left = lax.ppermute(
            parts[n - 2 - k], "chan", [(i, i - k) for i in range(k + 1, n)]
        )
        right = right + to_right.astype(f32)
        left = left + to_left.astype(f32)
    right = right.astype(bf16)
    left = left.astype(bf16)
    from_left = lax.ppermute(right, "chan", [(i, i + 1) for i in range(n - 1)])
    from_right = lax.ppermute(left, "chan", [(i + 1, i) for i in range(n - 1)])
    return from_left, from_right


def tm_gather(x, size, bits):
    dist = [0]
    for b in bits:
        got = lax.ppermute(x, "tm", [(i, i ^ (1 << b)) for i in range(size)])
        x = jnp.concatenate([x, got], axis=0)
        dist = dist + [d ^ (1 << b) for d in dist]
    got = lax.ppermute(x, "tm", [(i, i ^ 1) for i in range(size)])
    return x, got, dist


def prepare_kernel(dist, meta, gain, last_gain, ctc, *refs):
    ups, dns = refs[0:2], refs[2:4]
    up_t, dn_t, wide_gain, wide_last, ctc_t, up, usem, dsem = refs[4:]
    wide_gain[...] = jnp.broadcast_to(gain[...], wide_gain.shape)
    wide_last[...] = jnp.broadcast_to(last_gain[...], wide_last.shape)
    up_dist, dn_dist = dist
    tall = ups[0].shape[0] // len(up_dist)
    me = meta[1]

    def copies(srcs, dst, sem, dist):
        made = []
        for core in range(2):
            for q, d in enumerate(dist):
                row = pl.multiple_of(lax.bitwise_xor(me, d ^ core) * tall, 16)
                made.append(
                    pltpu.make_async_copy(
                        srcs[core].at[pl.ds(q * tall, tall)],
                        dst.at[pl.ds(row, tall)],
                        sem.at[core * len(dist) + q],
                    )
                )
        return made

    up_copies = copies(ups, up, usem, up_dist)
    dn_copies = copies(dns, dn_t, dsem, dn_dist)
    for c in up_copies + dn_copies:
        c.start()
    for i in range(0, ctc.shape[0], 256):
        ctc_t[:, i : i + 256] = ctc[i : i + 256, :].T
    for c in up_copies:
        c.wait()
    step = 256
    for i in range(0, up.shape[0], step):
        for j in range(0, up.shape[1], step):
            wide = min(step, up.shape[1] - j)
            up_t[j : j + wide, i : i + step] = up[i : i + step, j : j + wide].T
    for c in dn_copies:
        c.wait()


def prepare(meta, gain, last_gain, ctc, ups, dns, dist, width):
    hidden = ups[0].shape[1]
    count = 2 * len(dist[0])
    vmem = pl.BlockSpec(memory_space=pltpu.VMEM)
    anywhere = pl.BlockSpec(memory_space=pl.ANY)
    return pl.pallas_call(
        functools.partial(prepare_kernel, dist),
        out_shape=[
            jax.ShapeDtypeStruct((hidden, width), bf16),
            jax.ShapeDtypeStruct((width, hidden), bf16),
            jax.ShapeDtypeStruct((width, LANES), f32),
            jax.ShapeDtypeStruct((width, LANES), f32),
            jax.ShapeDtypeStruct(ctc.shape[::-1], bf16),
        ],
        in_specs=[pl.BlockSpec(memory_space=pltpu.SMEM)] + [vmem] * 3 + [anywhere] * 4,
        out_specs=[vmem] * 5,
        scratch_shapes=[
            pltpu.VMEM((width, hidden), bf16),
            pltpu.SemaphoreType.DMA((count,)),
            pltpu.SemaphoreType.DMA((count,)),
        ],
        compiler_params=pltpu.CompilerParams(vmem_limit_bytes=VMEM_LIMIT),
        cost_estimate=pl.CostEstimate(
            flops=0, bytes_accessed=8 * width * hidden, transcendentals=0
        ),
        name="prepare",
    )(meta, gain, last_gain, ctc, *ups, *dns)


def ffn_kernel(n, straight, meta, gain, up_t, dn_t, *refs):
    pieces = n if straight else 1 + 2 + 2 * (n - 2)
    xs = refs[:pieces]
    outs = refs[pieces : pieces + n]
    xin, xn, hid, terms, base, xsem, osem = refs[pieces + n :]
    width, rows = xin.shape
    feat = width // n
    fc = rows // n
    z = meta[0]
    for a in range(n):
        for here in range(n):

            @pl.when(z == here)
            def _(a=a, here=here):
                for r in range(n):
                    column = ((here + r) % n) * fc
                    pltpu.make_async_copy(
                        xs[piece_at(a, here, n, straight)].at[:, pl.ds(column, fc)],
                        xin.at[pl.ds(a * feat, feat), pl.ds(r * fc, fc)],
                        xsem.at[a * n + r],
                    ).start()


    hidden = up_t.shape[0]
    step = 256 if hidden % 256 == 0 else 128
    half = 256
    for start in range(0, rows, half):
        for r in range(start // fc, (start + half) // fc):
            for a in range(n):
                pltpu.make_async_copy(
                    xs[0].at[:, pl.ds(0, fc)],
                    xin.at[pl.ds(a * feat, feat), pl.ds(r * fc, fc)],
                    xsem.at[a * n + r],
                ).wait()
        for h in range(start, start + half, 128):
            x = xin[:, h : h + 128].astype(f32)
            mean = jnp.mean(x, axis=0, keepdims=True)
            var = jnp.mean(jnp.square(x - mean), axis=0, keepdims=True)
            normed = (x - mean) * lax.rsqrt(var + LN_EPSILON) * gain[...]
            xn[:, h : h + 128] = normed.astype(bf16)
        for j in range(0, hidden, step):
            a = jnp.dot(
                up_t[j : j + step, :], xn[:, start : start + half], preferred_element_type=f32
            )
            hid[j : j + step, start : start + half] = (a / (1.0 + jnp.exp(-a))).astype(bf16)
    copies = []
    for k, j in enumerate(range(0, width, 256)):
        p = [
            jnp.dot(
                dn_t[j : j + 256, :], hid[:, start : start + 256], preferred_element_type=f32
            )
            for start in range(0, rows, 256)
        ]
        for r in range(n):
            term = p[r * fc // 256][:, r * fc % 256 :][:, :fc]
            if r == 0:
                base[j : j + 256, :] = xin[j : j + 256, :fc].astype(f32) + 0.5 * term
                src = base.at[pl.ds(j, 256)]
            else:
                terms[r - 1, j : j + 256, :] = term.astype(bf16)
                src = terms.at[r - 1, pl.ds(j, 256)]
            copy = pltpu.make_async_copy(
                src, outs[(r - 1) % n].at[pl.ds(j, 256)], osem.at[k * n + r]
            )
            copy.start()
            copies.append(copy)
    for copy in copies:
        copy.wait()


def ffn(meta, gain, up_t, dn_t, xs, n, straight):
    _, rows = xs[0].shape
    fc = rows // n
    hidden, width = up_t.shape
    vmem = pl.BlockSpec(memory_space=pltpu.VMEM)
    anywhere = pl.BlockSpec(memory_space=pl.ANY)
    return pl.pallas_call(
        functools.partial(ffn_kernel, n, straight),
        out_shape=[jax.ShapeDtypeStruct((width, fc), bf16)] * (n - 1)
        + [jax.ShapeDtypeStruct((width, fc), f32)],
        in_specs=[pl.BlockSpec(memory_space=pltpu.SMEM)] + [vmem] * 3 + [anywhere] * len(xs),
        out_specs=[anywhere] * n,
        scratch_shapes=[
            pltpu.VMEM((width, rows), bf16),
            pltpu.VMEM((width, rows), bf16),
            pltpu.VMEM((hidden, rows), bf16),
            pltpu.VMEM((n - 1, width, fc), bf16),
            pltpu.VMEM((width, fc), f32),
            pltpu.SemaphoreType.DMA((n * n,)),
            pltpu.SemaphoreType.DMA((n * (width // 256),)),
        ],
        compiler_params=pltpu.CompilerParams(vmem_limit_bytes=FFN_VMEM),
        cost_estimate=pl.CostEstimate(
            flops=4 * rows * width * hidden,
            bytes_accessed=4 * width * hidden + 6 * rows * width,
            transcendentals=rows * hidden,
        ),
        name="ffn",
    )(meta, gain, up_t, dn_t, *xs)


def band_states(shard, starts, widths):
    prior = jnp.maximum(shard - 1, 0)
    start_in = jnp.where(shard > 0, starts[prior], 0)
    width_in = jnp.where(shard > 0, widths[prior], 2)
    return start_in, width_in, starts[shard], widths[shard]


def tail_kernel(first, last, meta, starts, widths, base, left, right, gain, ctc_t, label_rows, *refs):
    if not first:
        emitted, state_in, refs = refs[0], refs[1], refs[2:]
    emit, state_out, gaps = refs
    start_in, width_in, start_out, width_out = band_states(meta[2], starts, widths)

    residual = base[...] + 0.5 * (left[...].astype(f32) + right[...].astype(f32))
    mean = jnp.mean(residual, axis=0, keepdims=True)
    var = jnp.mean(jnp.square(residual - mean), axis=0, keepdims=True)
    wide = jnp.concatenate([gain[...]] * (residual.shape[1] // LANES), axis=1)
    normed = ((residual - mean) * lax.rsqrt(var + LN_EPSILON) * wide).astype(bf16)
    logits = jnp.dot(ctc_t[...], normed, preferred_element_type=f32)
    logits = logits - jnp.max(logits, axis=0, keepdims=True)
    emissions = (logits - jnp.log(jnp.sum(jnp.exp(logits), axis=0, keepdims=True))).T
    before = emit.shape[0] - emissions.shape[0]
    if before:
        emit[:before, :] = emitted[...]
    emit[before:, :] = emissions

    odd_start = lax.rem(start_in, 2)
    origin = start_in - odd_start
    row = start_in // RING
    after = jnp.minimum(row + 1, label_rows.shape[0] - 1)
    ring = row * RING + lax.broadcasted_iota(jnp.int32, (8, RING), 1)
    around = jnp.where(
        ring >= start_in,
        jnp.broadcast_to(label_rows[pl.ds(row, 1), :], (8, RING)),
        jnp.broadcast_to(label_rows[pl.ds(after, 1), :], (8, RING)),
    )
    lane = lax.broadcasted_iota(jnp.int32, (8, LANES), 1)
    sub = lax.broadcasted_iota(jnp.int32, (8, LANES), 0)
    spot = lax.rem(lane, LANE_STATES)
    block = lane // LANE_STATES
    odd_phases = list(range(1, PHASES, 2))

    shape = (RING, LANES * len(odd_phases))
    held = lax.broadcasted_iota(jnp.int32, shape, 1)
    held = origin + PHASES * lax.rem(held, LANE_STATES) + 2 * (held // LANES) + 1
    pick = lax.broadcasted_iota(jnp.int32, shape, 0) == lax.rem(held, RING)
    ids = jnp.dot(
        around.astype(f32).astype(bf16), pick.astype(f32).astype(bf16), preferred_element_type=f32
    ).astype(jnp.int32)
    ids_of = {p: ids[:, LANES * k : LANES * (k + 1)] for k, p in enumerate(odd_phases)}
    skip = {}
    for p in odd_phases:
        if p == 1:
            behind = pltpu.roll(ids_of[PHASES - 1], 1, axis=1)
        else:
            behind = ids_of[p - 2]
        skip[p] = (PHASES * spot + p - odd_start >= 2) & (ids_of[p] != behind)
    no_back = (spot == 0) & (odd_start == 0)
    no_rise = (spot == 0) & (odd_start == 1)

    vocab = emissions.shape[1]
    choose = (
        lax.broadcasted_iota(jnp.int32, (vocab, shape[1]), 0)
        == jnp.broadcast_to(ids[0:1], (vocab, shape[1]))
    )
    choose = choose.astype(f32).astype(bf16)
    rest = emissions
    picked = jnp.zeros((emissions.shape[0], shape[1]), f32)
    for _ in range(3):
        part = rest.astype(bf16)
        rest = rest - part.astype(f32)
        picked = picked + jnp.dot(part, choose, preferred_element_type=f32)
    blank = emissions[:, 0:1]
    gaps[...] = picked - blank
    blank_total = jnp.sum(blank)

    groups = BAND // (8 * LANE_ROWS)
    if first:
        rows = []
        for g in range(groups):
            entry = g * 8 * LANE_ROWS + 8 * block + sub
            for p in range(PHASES):
                state = origin + PHASES * spot + p
                live = (state >= start_in) & (state < start_in + jnp.minimum(width_in, BAND))
                rows.append(jnp.where(live & (lax.rem(state, BAND) == entry), 0.0, NEG_SCORE))
    else:
        rows = [state_in[k] for k in range(groups * PHASES)]

    def steps(t, rows):
        rows = list(rows)
        start = pl.multiple_of(t * 8, 8)
        tiles = {
            p: gaps[pl.ds(start, 8), LANES * k : LANES * (k + 1)] for k, p in enumerate(odd_phases)
        }
        for u in range(8):
            gap = {p: jnp.broadcast_to(tiles[p][u : u + 1], (8, LANES)) for p in odd_phases}
            for g in range(groups):
                was = rows[g * PHASES : (g + 1) * PHASES]
                now = list(was)
                back = jnp.where(no_back, NEG_SCORE, pltpu.roll(was[PHASES - 1], 1, axis=1))
                for p in range(0, PHASES, 2):
                    now[p] = jnp.maximum(was[p], back if p == 0 else was[p - 1])
                for p in odd_phases:
                    come = jnp.where(skip[p], now[p - 1], was[p - 1])
                    if p == 1:
                        come = jnp.where(no_rise, NEG_SCORE, come)
                    now[p] = jnp.maximum(was[p], come) + gap[p]
                rows[g * PHASES : (g + 1) * PHASES] = now
        return tuple(rows)

    rows = lax.fori_loop(0, emissions.shape[0] // 8, steps, tuple(rows))
    if not last:
        for k in range(groups * PHASES):
            state_out[k] = rows[k] + blank_total
        return

    stack = jnp.concatenate(
        [
            jnp.concatenate([rows[g * PHASES + p] for p in range(PHASES)], axis=1)
            for g in range(groups)
        ],
        axis=0,
    )
    parts = []
    for _ in range(3):
        part = stack.astype(bf16)
        stack = stack - part.astype(f32)
        parts.append(part.astype(f32))
    parts = jnp.concatenate(parts, axis=0).astype(bf16)
    count = groups * 8
    where = lax.broadcasted_iota(jnp.int32, (PHASES * LANES, 1), 0)
    slot = lax.rem(where, LANES)
    state = origin + PHASES * lax.rem(slot, LANE_STATES) + where // LANES
    owner = slot // LANE_STATES
    beyond = (state == origin) & (odd_start == 1)
    state = jnp.where(beyond, origin + RING, state)
    owner = jnp.where(beyond, lax.rem(owner + LANE_ROWS - 1, LANE_ROWS), owner)
    leaves = (state >= start_out) & (state < start_out + BAND)
    column = jnp.where(leaves, lax.rem(state, BAND), -1)
    wanted = lax.broadcasted_iota(jnp.int32, (PHASES * LANES, BAND), 1)
    exit_residue = lax.broadcasted_iota(jnp.int32, (8, BAND), 1)
    ahead = lax.rem(exit_residue - lax.rem(start_out, BAND) + BAND, BAND)
    for e in range(LANE_ROWS):
        take = jnp.where(owner == e, column, -1) == wanted
        got = jnp.dot(parts, take.astype(f32).astype(bf16), preferred_element_type=f32)
        got = got[:count] + got[count : 2 * count] + got[2 * count :]
        for g in range(groups):
            first_row = g * 8 * LANE_ROWS + 8 * e
            state_out[first_row : first_row + 8, :] = jnp.where(
                ahead < width_out, got[8 * g : 8 * g + 8] + blank_total, NEG_SCORE
            )


def tail(first, last, meta, starts, widths, base, left, right, gain, ctc_t, label_rows, *state):
    fc = base.shape[1]
    vocab = ctc_t.shape[0]
    smem = pl.BlockSpec(memory_space=pltpu.SMEM)
    vmem = pl.BlockSpec(memory_space=pltpu.VMEM)
    shape = (BAND, BAND) if last else (RING * BAND // (8 * LANES), 8, LANES)
    return pl.pallas_call(
        functools.partial(tail_kernel, first, last),
        out_shape=[
            jax.ShapeDtypeStruct((fc + (0 if first else state[0].shape[0]), vocab), f32),
            jax.ShapeDtypeStruct(shape, f32),
        ],
        in_specs=[smem] * 3 + [vmem] * (6 + len(state)),
        out_specs=[vmem] * 2,
        scratch_shapes=[pltpu.VMEM((fc, LANES * PHASES // 2), f32)],
        compiler_params=pltpu.CompilerParams(vmem_limit_bytes=VMEM_LIMIT),
        cost_estimate=pl.CostEstimate(
            flops=40 * fc * BAND * BAND, bytes_accessed=16 * fc * gain.shape[0], transcendentals=fc * vocab
        ),
        name="tail",
    )(meta, starts, widths, base, left, right, gain, ctc_t, label_rows, *state)


def product_kernel(mats, out, left):
    groups = BAND // 8
    out[...] = mats[0]

    def lap(k, _):
        left[...] = out[...]
        acc = [jnp.full((8, BAND), 64 * NEG_SCORE, f32) for _ in range(groups)]
        for j in range(0, BAND, 8):
            later = mats[k, j : j + 8, :]
            for u in range(8):
                row = jnp.broadcast_to(later[u : u + 1], (8, BAND))
                for g in range(groups):
                    col = left[8 * g : 8 * g + 8, j + u : j + u + 1]
                    acc[g] = jnp.maximum(acc[g], jnp.broadcast_to(col, (8, BAND)) + row)
        for g in range(groups):
            out[8 * g : 8 * g + 8, :] = acc[g]
        return 0

    lax.fori_loop(1, mats.shape[0], lap, 0)


def product(mats):
    vmem = pl.BlockSpec(memory_space=pltpu.VMEM)
    return pl.pallas_call(
        product_kernel,
        out_shape=jax.ShapeDtypeStruct((BAND, BAND), f32),
        in_specs=[vmem],
        out_specs=vmem,
        scratch_shapes=[pltpu.VMEM((BAND, BAND), f32)],
        compiler_params=pltpu.CompilerParams(vmem_limit_bytes=VMEM_LIMIT),
        name="product",
    )(mats)


def score_kernel(scale, meta, starts, widths, near, far, out):
    z = meta[0]
    me = meta[1]
    _, _, start_out, width_out = band_states(meta[2], starts, widths)
    sub = lax.broadcasted_iota(jnp.int32, (BAND, BAND), 0)
    lane = lax.broadcasted_iota(jnp.int32, (BAND, BAND), 1)

    def through(col, mat):
        return jnp.max(col + mat, axis=0, keepdims=True)

    def turn(row):
        return jnp.max(
            jnp.where(sub == lane, jnp.broadcast_to(row, (BAND, BAND)), 64 * NEG_SCORE),
            axis=1,
            keepdims=True,
        )

    place = lax.broadcasted_iota(jnp.int32, (BAND, 1), 0)
    col = jnp.where(place < 2, 0.0, NEG_SCORE).astype(f32)
    col = lax.fori_loop(0, me, lambda g, c: turn(through(c, far[g])), col)
    col = lax.fori_loop(0, z, lambda k, c: turn(through(c, near[k])), col)
    col = turn(through(col, near[z]))
    home = lax.rem(start_out + lane, BAND)
    best = jnp.max(jnp.where(sub == home, col, 64 * NEG_SCORE), axis=0, keepdims=True)
    live = lax.broadcasted_iota(jnp.int32, (1, BAND), 1) < width_out
    out[...] = jnp.where(live, best * scale, 0.0)


def scores(scale, meta, starts, widths, near, far):
    smem = pl.BlockSpec(memory_space=pltpu.SMEM)
    vmem = pl.BlockSpec(memory_space=pltpu.VMEM)
    return pl.pallas_call(
        functools.partial(score_kernel, scale),
        out_shape=jax.ShapeDtypeStruct((1, BAND), f32),
        in_specs=[smem] * 3 + [vmem] * 2,
        out_specs=vmem,
        compiler_params=pltpu.CompilerParams(vmem_limit_bytes=VMEM_LIMIT),
        name="scores",
    )(meta, starts, widths, near, far)


def compute(frames, up_weight, down_weight, ffn_gain, final_gain, ctc_weight, labels, starts, widths):
    n = lax.axis_size("chan")
    z = lax.axis_index("chan")
    size = lax.axis_size("tm")
    me = lax.axis_index("tm")
    rows, feat = frames.shape
    fd = rows // n
    fc = fd // CHUNKS
    shard = me * n + z
    meta = jnp.stack([z, me, shard]).astype(jnp.int32)
    high = list(range(1, size.bit_length() - 1))
    label_rows = labels.reshape(-1, RING)
    gain = ffn_gain.reshape(-1, 1)
    last_gain = final_gain.reshape(-1, 1)

    turned = frames.T
    gathered = []
    for c in range(CHUNKS):
        cuts = [turned[:, (d * CHUNKS + c) * fc :][:, :fc] for d in range(n)]
        cut = jnp.concatenate(cuts, axis=1)
        gathered.append(turn_gather(cut, n) if c else line_gather(cut, n))
    up_own, up_other, dist = tm_gather(up_weight, size, high)
    dn_own, dn_other, dn_dist = tm_gather(down_weight.T, size, high[::-1])
    up_t, dn_t, gain, last_gain, ctc_t = prepare(
        meta, gain, last_gain, ctc_weight, (up_own, up_other), (dn_own, dn_other), (dist, dn_dist), n * feat
    )

    state = emissions = ()
    for c in range(CHUNKS):
        *parts, base = ffn(meta, gain, up_t, dn_t, gathered[c], n, c > 0)
        from_left, from_right = line_scatter(parts, n)
        emissions, state = tail(
            c == 0,
            c == CHUNKS - 1,
            meta,
            starts,
            widths,
            base,
            from_left,
            from_right,
            last_gain,
            ctc_t,
            label_rows,
            *((emissions, state) if c else ()),
        )

    near = lax.all_gather(state, "chan")
    far = lax.all_gather(product(near), "tm")
    band_row = scores(1.0 / (rows * size), meta, starts, widths, near, far)
    return emissions, band_row


def solution(mesh):
    in_specs = (P("tm", "chan"), P("tm", "chan"), P("chan", "tm"), P(), P(), P(), P(), P(), P())
    out_specs = (P(("tm", "chan"), None), P(("tm", "chan"), None))
    return jax.shard_map(compute, mesh=mesh, in_specs=in_specs, out_specs=out_specs, check_vma=False)
```

```python
import functools

import jax
import jax.numpy as jnp
from jax import lax
from jax.experimental import pallas as pl
from jax.experimental.pallas import tpu as pltpu
from jax.sharding import PartitionSpec as P


BAND = 128
RING = 2 * BAND
LANES = 128
PHASES = 8
LANE_STATES = RING // PHASES
LANE_ROWS = LANES // LANE_STATES
LN_EPSILON = 1e-05
NEG_SCORE = -1000000000.0
CHUNKS = 2
VMEM_LIMIT = 24 * 1024 * 1024
FFN_VMEM = 28 * 1024 * 1024


f32 = jnp.float32
bf16 = jnp.bfloat16


def turn_gather(x, n):
    got = [x]
    for k in range(1, n):
        got.append(lax.ppermute(x, "chan", [(i, (i + k) % n) for i in range(n)]))
    return got


def line_gather(x, n):
    r1 = lax.ppermute(x, "chan", [(i, i + 1) for i in range(n - 1)])
    l1 = lax.ppermute(x, "chan", [(i + 1, i) for i in range(n - 1)])
    r2 = []
    l2 = []
    for k in range(1, n - 1):
        r2.append(lax.ppermute(r1, "chan", [(i, i + k) for i in range(1, n - k)]))
        l2.append(lax.ppermute(l1, "chan", [(i, i - k) for i in range(k, n - 1)]))
    return [x, r1, l1, *r2, *l2]


def piece_at(a, z, n, straight):
    if straight:
        return (z - a) % n
    if a == z:
        return 0
    if a == z - 1:
        return 1
    if a == z + 1:
        return 2
    if a < z:
        return 3 + (z - a - 1) - 1
    return 3 + (n - 2) + (a - z - 1) - 1


def line_scatter(parts, n):
    right = parts[0].astype(f32)
    left = parts[n - 2].astype(f32)
    for k in range(1, n - 1):
        to_right = lax.ppermute(parts[k], "chan", [(i, i + k) for i in range(0, n - 1 - k)])
        to_left = lax.ppermute(
            parts[n - 2 - k], "chan", [(i, i - k) for i in range(k + 1, n)]
        )
        right = right + to_right.astype(f32)
        left = left + to_left.astype(f32)
    right = right.astype(bf16)
    left = left.astype(bf16)
    from_left = lax.ppermute(right, "chan", [(i, i + 1) for i in range(n - 1)])
    from_right = lax.ppermute(left, "chan", [(i + 1, i) for i in range(n - 1)])
    return from_left, from_right


def tm_gather(x, size, bits):
    dist = [0]
    for b in bits:
        got = lax.ppermute(x, "tm", [(i, i ^ (1 << b)) for i in range(size)])
        x = jnp.concatenate([x, got], axis=0)
        dist = dist + [d ^ (1 << b) for d in dist]
    got = lax.ppermute(x, "tm", [(i, i ^ 1) for i in range(size)])
    return x, got, dist


def prepare_kernel(dist, meta, gain, last_gain, ctc, *refs):
    ups, dns = refs[0:2], refs[2:4]
    up_t, dn_t, wide_gain, wide_last, ctc_t, up, usem, dsem = refs[4:]
    wide_gain[...] = jnp.broadcast_to(gain[...], wide_gain.shape)
    wide_last[...] = jnp.broadcast_to(last_gain[...], wide_last.shape)
    up_dist, dn_dist = dist
    tall = ups[0].shape[0] // len(up_dist)
    me = meta[1]

    def copies(srcs, dst, sem, dist):
        made = []
        for core in range(2):
            for q, d in enumerate(dist):
                row = pl.multiple_of(lax.bitwise_xor(me, d ^ core) * tall, 16)
                made.append(
                    pltpu.make_async_copy(
                        srcs[core].at[pl.ds(q * tall, tall)],
                        dst.at[pl.ds(row, tall)],
                        sem.at[core * len(dist) + q],
                    )
                )
        return made

    up_copies = copies(ups, up, usem, up_dist)
    dn_copies = copies(dns, dn_t, dsem, dn_dist)
    for c in up_copies + dn_copies:
        c.start()
    for i in range(0, ctc.shape[0], 256):
        ctc_t[:, i : i + 256] = ctc[i : i + 256, :].T
    for c in up_copies:
        c.wait()
    step = 256
    for i in range(0, up.shape[0], step):
        for j in range(0, up.shape[1], step):
            wide = min(step, up.shape[1] - j)
            up_t[j : j + wide, i : i + step] = up[i : i + step, j : j + wide].T
    for c in dn_copies:
        c.wait()


def prepare(meta, gain, last_gain, ctc, ups, dns, dist, width):
    hidden = ups[0].shape[1]
    count = 2 * len(dist[0])
    vmem = pl.BlockSpec(memory_space=pltpu.VMEM)
    anywhere = pl.BlockSpec(memory_space=pl.ANY)
    return pl.pallas_call(
        functools.partial(prepare_kernel, dist),
        out_shape=[
            jax.ShapeDtypeStruct((hidden, width), bf16),
            jax.ShapeDtypeStruct((width, hidden), bf16),
            jax.ShapeDtypeStruct((width, LANES), f32),
            jax.ShapeDtypeStruct((width, LANES), f32),
            jax.ShapeDtypeStruct(ctc.shape[::-1], bf16),
        ],
        in_specs=[pl.BlockSpec(memory_space=pltpu.SMEM)] + [vmem] * 3 + [anywhere] * 4,
        out_specs=[vmem] * 5,
        scratch_shapes=[
            pltpu.VMEM((width, hidden), bf16),
            pltpu.SemaphoreType.DMA((count,)),
            pltpu.SemaphoreType.DMA((count,)),
        ],
        compiler_params=pltpu.CompilerParams(vmem_limit_bytes=VMEM_LIMIT),
        cost_estimate=pl.CostEstimate(
            flops=0, bytes_accessed=8 * width * hidden, transcendentals=0
        ),
        name="prepare",
    )(meta, gain, last_gain, ctc, *ups, *dns)


def ffn_kernel(n, straight, meta, gain, up_t, dn_t, *refs):
    pieces = n if straight else 1 + 2 + 2 * (n - 2)
    xs = refs[:pieces]
    outs = refs[pieces : pieces + n]
    xin, xn, hid, terms, base, xsem, osem = refs[pieces + n :]
    width, rows = xin.shape
    feat = width // n
    fc = rows // n
    z = meta[0]
    for a in range(n):
        for here in range(n):

            @pl.when(z == here)
            def _(a=a, here=here):
                for r in range(n):
                    column = ((here + r) % n) * fc
                    pltpu.make_async_copy(
                        xs[piece_at(a, here, n, straight)].at[:, pl.ds(column, fc)],
                        xin.at[pl.ds(a * feat, feat), pl.ds(r * fc, fc)],
                        xsem.at[a * n + r],
                    ).start()


    hidden = up_t.shape[0]
    step = 256 if hidden % 256 == 0 else 128
    half = 256
    for start in range(0, rows, half):
        for r in range(start // fc, (start + half) // fc):
            for a in range(n):
                pltpu.make_async_copy(
                    xs[0].at[:, pl.ds(0, fc)],
                    xin.at[pl.ds(a * feat, feat), pl.ds(r * fc, fc)],
                    xsem.at[a * n + r],
                ).wait()
        for h in range(start, start + half, 128):
            x = xin[:, h : h + 128].astype(f32)
            mean = jnp.mean(x, axis=0, keepdims=True)
            var = jnp.mean(jnp.square(x - mean), axis=0, keepdims=True)
            normed = (x - mean) * lax.rsqrt(var + LN_EPSILON) * gain[...]
            xn[:, h : h + 128] = normed.astype(bf16)
        for j in range(0, hidden, step):
            a = jnp.dot(
                up_t[j : j + step, :], xn[:, start : start + half], preferred_element_type=f32
            )
            hid[j : j + step, start : start + half] = (a / (1.0 + jnp.exp(-a))).astype(bf16)
    copies = []
    for k, j in enumerate(range(0, width, 256)):
        p = [
            jnp.dot(
                dn_t[j : j + 256, :], hid[:, start : start + 256], preferred_element_type=f32
            )
            for start in range(0, rows, 256)
        ]
        for r in range(n):
            term = p[r * fc // 256][:, r * fc % 256 :][:, :fc]
            if r == 0:
                base[j : j + 256, :] = xin[j : j + 256, :fc].astype(f32) + 0.5 * term
                src = base.at[pl.ds(j, 256)]
            else:
                terms[r - 1, j : j + 256, :] = term.astype(bf16)
                src = terms.at[r - 1, pl.ds(j, 256)]
            copy = pltpu.make_async_copy(
                src, outs[(r - 1) % n].at[pl.ds(j, 256)], osem.at[k * n + r]
            )
            copy.start()
            copies.append(copy)
    for copy in copies:
        copy.wait()


def ffn(meta, gain, up_t, dn_t, xs, n, straight):
    _, rows = xs[0].shape
    fc = rows // n
    hidden, width = up_t.shape
    vmem = pl.BlockSpec(memory_space=pltpu.VMEM)
    anywhere = pl.BlockSpec(memory_space=pl.ANY)
    return pl.pallas_call(
        functools.partial(ffn_kernel, n, straight),
        out_shape=[jax.ShapeDtypeStruct((width, fc), bf16)] * (n - 1)
        + [jax.ShapeDtypeStruct((width, fc), f32)],
        in_specs=[pl.BlockSpec(memory_space=pltpu.SMEM)] + [vmem] * 3 + [anywhere] * len(xs),
        out_specs=[anywhere] * n,
        scratch_shapes=[
            pltpu.VMEM((width, rows), bf16),
            pltpu.VMEM((width, rows), bf16),
            pltpu.VMEM((hidden, rows), bf16),
            pltpu.VMEM((n - 1, width, fc), bf16),
            pltpu.VMEM((width, fc), f32),
            pltpu.SemaphoreType.DMA((n * n,)),
            pltpu.SemaphoreType.DMA((n * (width // 256),)),
        ],
        compiler_params=pltpu.CompilerParams(vmem_limit_bytes=FFN_VMEM),
        cost_estimate=pl.CostEstimate(
            flops=4 * rows * width * hidden,
            bytes_accessed=4 * width * hidden + 6 * rows * width,
            transcendentals=rows * hidden,
        ),
        name="ffn",
    )(meta, gain, up_t, dn_t, *xs)


def band_states(shard, starts, widths):
    prior = jnp.maximum(shard - 1, 0)
    start_in = jnp.where(shard > 0, starts[prior], 0)
    width_in = jnp.where(shard > 0, widths[prior], 2)
    return start_in, width_in, starts[shard], widths[shard]


def tail_kernel(first, last, meta, starts, widths, base, left, right, gain, ctc_t, label_rows, *refs):
    if not first:
        emitted, state_in, refs = refs[0], refs[1], refs[2:]
    emit, state_out, gaps = refs
    start_in, width_in, start_out, width_out = band_states(meta[2], starts, widths)

    residual = base[...] + 0.5 * (left[...].astype(f32) + right[...].astype(f32))
    mean = jnp.mean(residual, axis=0, keepdims=True)
    var = jnp.mean(jnp.square(residual - mean), axis=0, keepdims=True)
    wide = jnp.concatenate([gain[...]] * (residual.shape[1] // LANES), axis=1)
    normed = ((residual - mean) * lax.rsqrt(var + LN_EPSILON) * wide).astype(bf16)
    logits = jnp.dot(ctc_t[...], normed, preferred_element_type=f32)
    logits = logits - jnp.max(logits, axis=0, keepdims=True)
    emissions = (logits - jnp.log(jnp.sum(jnp.exp(logits), axis=0, keepdims=True))).T
    before = emit.shape[0] - emissions.shape[0]
    if before:
        emit[:before, :] = emitted[...]
    emit[before:, :] = emissions

    odd_start = lax.rem(start_in, 2)
    origin = start_in - odd_start
    row = start_in // RING
    after = jnp.minimum(row + 1, label_rows.shape[0] - 1)
    ring = row * RING + lax.broadcasted_iota(jnp.int32, (8, RING), 1)
    around = jnp.where(
        ring >= start_in,
        jnp.broadcast_to(label_rows[pl.ds(row, 1), :], (8, RING)),
        jnp.broadcast_to(label_rows[pl.ds(after, 1), :], (8, RING)),
    )
    lane = lax.broadcasted_iota(jnp.int32, (8, LANES), 1)
    sub = lax.broadcasted_iota(jnp.int32, (8, LANES), 0)
    spot = lax.rem(lane, LANE_STATES)
    block = lane // LANE_STATES
    odd_phases = list(range(1, PHASES, 2))

    shape = (RING, LANES * len(odd_phases))
    held = lax.broadcasted_iota(jnp.int32, shape, 1)
    held = origin + PHASES * lax.rem(held, LANE_STATES) + 2 * (held // LANES) + 1
    pick = lax.broadcasted_iota(jnp.int32, shape, 0) == lax.rem(held, RING)
    ids = jnp.dot(
        around.astype(f32).astype(bf16), pick.astype(f32).astype(bf16), preferred_element_type=f32
    ).astype(jnp.int32)
    ids_of = {p: ids[:, LANES * k : LANES * (k + 1)] for k, p in enumerate(odd_phases)}
    skip = {}
    for p in odd_phases:
        if p == 1:
            behind = pltpu.roll(ids_of[PHASES - 1], 1, axis=1)
        else:
            behind = ids_of[p - 2]
        skip[p] = (PHASES * spot + p - odd_start >= 2) & (ids_of[p] != behind)
    no_back = (spot == 0) & (odd_start == 0)
    no_rise = (spot == 0) & (odd_start == 1)

    vocab = emissions.shape[1]
    choose = (
        lax.broadcasted_iota(jnp.int32, (vocab, shape[1]), 0)
        == jnp.broadcast_to(ids[0:1], (vocab, shape[1]))
    )
    choose = choose.astype(f32).astype(bf16)
    rest = emissions
    picked = jnp.zeros((emissions.shape[0], shape[1]), f32)
    for _ in range(3):
        part = rest.astype(bf16)
        rest = rest - part.astype(f32)
        picked = picked + jnp.dot(part, choose, preferred_element_type=f32)
    blank = emissions[:, 0:1]
    gaps[...] = picked - blank
    blank_total = jnp.sum(blank)

    groups = BAND // (8 * LANE_ROWS)
    if first:
        rows = []
        for g in range(groups):
            entry = g * 8 * LANE_ROWS + 8 * block + sub
            for p in range(PHASES):
                state = origin + PHASES * spot + p
                live = (state >= start_in) & (state < start_in + jnp.minimum(width_in, BAND))
                rows.append(jnp.where(live & (lax.rem(state, BAND) == entry), 0.0, NEG_SCORE))
    else:
        rows = [state_in[k] for k in range(groups * PHASES)]

    def steps(t, rows):
        rows = list(rows)
        start = pl.multiple_of(t * 8, 8)
        tiles = {
            p: gaps[pl.ds(start, 8), LANES * k : LANES * (k + 1)] for k, p in enumerate(odd_phases)
        }
        for u in range(8):
            gap = {p: jnp.broadcast_to(tiles[p][u : u + 1], (8, LANES)) for p in odd_phases}
            for g in range(groups):
                was = rows[g * PHASES : (g + 1) * PHASES]
                now = list(was)
                back = jnp.where(no_back, NEG_SCORE, pltpu.roll(was[PHASES - 1], 1, axis=1))
                for p in range(0, PHASES, 2):
                    now[p] = jnp.maximum(was[p], back if p == 0 else was[p - 1])
                for p in odd_phases:
                    come = jnp.where(skip[p], now[p - 1], was[p - 1])
                    if p == 1:
                        come = jnp.where(no_rise, NEG_SCORE, come)
                    now[p] = jnp.maximum(was[p], come) + gap[p]
                rows[g * PHASES : (g + 1) * PHASES] = now
        return tuple(rows)

    rows = lax.fori_loop(0, emissions.shape[0] // 8, steps, tuple(rows))
    if not last:
        for k in range(groups * PHASES):
            state_out[k] = rows[k] + blank_total
        return

    stack = jnp.concatenate(
        [
            jnp.concatenate([rows[g * PHASES + p] for p in range(PHASES)], axis=1)
            for g in range(groups)
        ],
        axis=0,
    )
    parts = []
    for _ in range(3):
        part = stack.astype(bf16)
        stack = stack - part.astype(f32)
        parts.append(part.astype(f32))
    parts = jnp.concatenate(parts, axis=0).astype(bf16)
    count = groups * 8
    where = lax.broadcasted_iota(jnp.int32, (PHASES * LANES, 1), 0)
    slot = lax.rem(where, LANES)
    state = origin + PHASES * lax.rem(slot, LANE_STATES) + where // LANES
    owner = slot // LANE_STATES
    beyond = (state == origin) & (odd_start == 1)
    state = jnp.where(beyond, origin + RING, state)
    owner = jnp.where(beyond, lax.rem(owner + LANE_ROWS - 1, LANE_ROWS), owner)
    leaves = (state >= start_out) & (state < start_out + BAND)
    column = jnp.where(leaves, lax.rem(state, BAND), -1)
    wanted = lax.broadcasted_iota(jnp.int32, (PHASES * LANES, BAND), 1)
    exit_residue = lax.broadcasted_iota(jnp.int32, (8, BAND), 1)
    ahead = lax.rem(exit_residue - lax.rem(start_out, BAND) + BAND, BAND)
    for e in range(LANE_ROWS):
        take = jnp.where(owner == e, column, -1) == wanted
        got = jnp.dot(parts, take.astype(f32).astype(bf16), preferred_element_type=f32)
        got = got[:count] + got[count : 2 * count] + got[2 * count :]
        for g in range(groups):
            first_row = g * 8 * LANE_ROWS + 8 * e
            state_out[first_row : first_row + 8, :] = jnp.where(
                ahead < width_out, got[8 * g : 8 * g + 8] + blank_total, NEG_SCORE
            )


def tail(first, last, meta, starts, widths, base, left, right, gain, ctc_t, label_rows, *state):
    fc = base.shape[1]
    vocab = ctc_t.shape[0]
    smem = pl.BlockSpec(memory_space=pltpu.SMEM)
    vmem = pl.BlockSpec(memory_space=pltpu.VMEM)
    shape = (BAND, BAND) if last else (RING * BAND // (8 * LANES), 8, LANES)
    return pl.pallas_call(
        functools.partial(tail_kernel, first, last),
        out_shape=[
            jax.ShapeDtypeStruct((fc + (0 if first else state[0].shape[0]), vocab), f32),
            jax.ShapeDtypeStruct(shape, f32),
        ],
        in_specs=[smem] * 3 + [vmem] * (6 + len(state)),
        out_specs=[vmem] * 2,
        scratch_shapes=[pltpu.VMEM((fc, LANES * PHASES // 2), f32)],
        compiler_params=pltpu.CompilerParams(vmem_limit_bytes=VMEM_LIMIT),
        cost_estimate=pl.CostEstimate(
            flops=40 * fc * BAND * BAND, bytes_accessed=16 * fc * gain.shape[0], transcendentals=fc * vocab
        ),
        name="tail",
    )(meta, starts, widths, base, left, right, gain, ctc_t, label_rows, *state)


def product_kernel(n, meta, *refs):
    got = refs[:n]
    out, mats, left = refs[n:]
    groups = BAND // 8
    for k in range(n):
        mats[lax.rem(meta[0] + n - k, n)] = got[k][...]
    out[...] = mats[0]

    def lap(k, _):
        left[...] = out[...]
        acc = [jnp.full((8, BAND), 64 * NEG_SCORE, f32) for _ in range(groups)]
        for j in range(0, BAND, 8):
            later = mats[k, j : j + 8, :]
            for u in range(8):
                row = jnp.broadcast_to(later[u : u + 1], (8, BAND))
                for g in range(groups):
                    col = left[8 * g : 8 * g + 8, j + u : j + u + 1]
                    acc[g] = jnp.maximum(acc[g], jnp.broadcast_to(col, (8, BAND)) + row)
        for g in range(groups):
            out[8 * g : 8 * g + 8, :] = acc[g]
        return 0

    lax.fori_loop(1, n, lap, 0)


def product(meta, got):
    n = len(got)
    vmem = pl.BlockSpec(memory_space=pltpu.VMEM)
    return pl.pallas_call(
        functools.partial(product_kernel, n),
        out_shape=[
            jax.ShapeDtypeStruct((BAND, BAND), f32),
            jax.ShapeDtypeStruct((n, BAND, BAND), f32),
        ],
        in_specs=[pl.BlockSpec(memory_space=pltpu.SMEM)] + [vmem] * n,
        out_specs=[vmem] * 2,
        scratch_shapes=[pltpu.VMEM((BAND, BAND), f32)],
        compiler_params=pltpu.CompilerParams(vmem_limit_bytes=VMEM_LIMIT),
        name="product",
    )(meta, *got)


def score_kernel(scale, meta, starts, widths, near, far, out):
    z = meta[0]
    me = meta[1]
    _, _, start_out, width_out = band_states(meta[2], starts, widths)
    sub = lax.broadcasted_iota(jnp.int32, (BAND, BAND), 0)
    lane = lax.broadcasted_iota(jnp.int32, (BAND, BAND), 1)

    def through(col, mat):
        return jnp.max(col + mat, axis=0, keepdims=True)

    def turn(row):
        return jnp.max(
            jnp.where(sub == lane, jnp.broadcast_to(row, (BAND, BAND)), 64 * NEG_SCORE),
            axis=1,
            keepdims=True,
        )

    place = lax.broadcasted_iota(jnp.int32, (BAND, 1), 0)
    col = jnp.where(place < 2, 0.0, NEG_SCORE).astype(f32)
    col = lax.fori_loop(0, me, lambda g, c: turn(through(c, far[g])), col)
    col = lax.fori_loop(0, z, lambda k, c: turn(through(c, near[k])), col)
    col = turn(through(col, near[z]))
    home = lax.rem(start_out + lane, BAND)
    best = jnp.max(jnp.where(sub == home, col, 64 * NEG_SCORE), axis=0, keepdims=True)
    live = lax.broadcasted_iota(jnp.int32, (1, BAND), 1) < width_out
    out[...] = jnp.where(live, best * scale, 0.0)


def scores(scale, meta, starts, widths, near, far):
    smem = pl.BlockSpec(memory_space=pltpu.SMEM)
    vmem = pl.BlockSpec(memory_space=pltpu.VMEM)
    return pl.pallas_call(
        functools.partial(score_kernel, scale),
        out_shape=jax.ShapeDtypeStruct((1, BAND), f32),
        in_specs=[smem] * 3 + [vmem] * 2,
        out_specs=vmem,
        compiler_params=pltpu.CompilerParams(vmem_limit_bytes=VMEM_LIMIT),
        name="scores",
    )(meta, starts, widths, near, far)


def compute(frames, up_weight, down_weight, ffn_gain, final_gain, ctc_weight, labels, starts, widths):
    n = lax.axis_size("chan")
    z = lax.axis_index("chan")
    size = lax.axis_size("tm")
    me = lax.axis_index("tm")
    rows, feat = frames.shape
    fd = rows // n
    fc = fd // CHUNKS
    shard = me * n + z
    meta = jnp.stack([z, me, shard]).astype(jnp.int32)
    high = list(range(1, size.bit_length() - 1))
    label_rows = labels.reshape(-1, RING)
    gain = ffn_gain.reshape(-1, 1)
    last_gain = final_gain.reshape(-1, 1)

    turned = frames.T
    gathered = []
    for c in range(CHUNKS):
        cuts = [turned[:, (d * CHUNKS + c) * fc :][:, :fc] for d in range(n)]
        cut = jnp.concatenate(cuts, axis=1)
        gathered.append(turn_gather(cut, n) if c else line_gather(cut, n))
    up_own, up_other, dist = tm_gather(up_weight, size, high)
    dn_own, dn_other, dn_dist = tm_gather(down_weight.T, size, high[::-1])
    up_t, dn_t, gain, last_gain, ctc_t = prepare(
        meta, gain, last_gain, ctc_weight, (up_own, up_other), (dn_own, dn_other), (dist, dn_dist), n * feat
    )

    state = emissions = ()
    for c in range(CHUNKS):
        *parts, base = ffn(meta, gain, up_t, dn_t, gathered[c], n, c > 0)
        from_left, from_right = line_scatter(parts, n)
        emissions, state = tail(
            c == 0,
            c == CHUNKS - 1,
            meta,
            starts,
            widths,
            base,
            from_left,
            from_right,
            last_gain,
            ctc_t,
            label_rows,
            *((emissions, state) if c else ()),
        )

    whole, near = product(meta, turn_gather(state, n))
    far = lax.all_gather(whole, "tm")
    band_row = scores(1.0 / (rows * size), meta, starts, widths, near, far)
    return emissions, band_row


def solution(mesh):
    in_specs = (P("tm", "chan"), P("tm", "chan"), P("chan", "tm"), P(), P(), P(), P(), P(), P())
    out_specs = (P(("tm", "chan"), None), P(("tm", "chan"), None))
    return jax.shard_map(compute, mesh=mesh, in_specs=in_specs, out_specs=out_specs, check_vma=False)
```
